512 devices in a mesh: rows: 64 (over z, y), cols: 8 (over x, core).
Axes of the slice: x: 4, y: 4, z: 16, core: 2. Of those that a mesh axis runs over, the one named last changes fastest.
Arguments:
- x_start: float32 [96, 32768], P('cols', 'rows'), may hold values from -6 to 6
- p_start: float32 [96, 32768], P('cols', 'rows'), may hold values from -6 to 6
- k_diag: bfloat16 [512, 64, 64], P('rows'), as said below
- k_link: bfloat16 [512, 4, 64, 64], P('rows')
- m_diag: bfloat16 [512, 64, 64], P('rows'), as said below
- m_link: bfloat16 [512, 4, 64, 64], P('rows')
- link_to: int32 [512, 4], P('rows'), may hold values from 0 to 7, as said below
- link_count: int32 [512], P('rows'), may hold values from 1 to 4, as said below
- k_iface: bfloat16 [64, 64, 3, 64, 64], P('rows'), as said below
- m_iface: bfloat16 [64, 64, 3, 64, 64], P('rows'), as said below
- iface_local: int32 [64, 64, 3], P('rows'), may hold values from 0 to 7, as said below
- iface_live: int32 [64, 64, 3], P('rows'), may hold values from 0 to 1, as said below
Outputs:
- x_out: float32 [96, 32768], P('cols', 'rows')
- p_out: float32 [96, 32768], P('cols', 'rows')
- ritz: float32 [96, 96], replicated
The draws below stay inside these ranges and needn't reach their ends.
Inputs may be any that keep to these rules, and one draw needn't show every extreme that they name: `link_to`: for each row owner and each b < 4, the b-th links of its 8 supernodes form a permutation of its supernodes. `link_count`: the first supernode of every row owner has all 4 links live. `iface_local`: each row owner's 192 slots name each of its supernodes at most (199) // 8 times. iface_live[p, q, c] = iface_live[q, p, c], and it is 0 where p = q. `k_iface`: for p < q the block for (q, p, c) is the transpose of the block for (p, q, c). `m_iface`: for p < q the block for (q, p, c) is the transpose of the block for (p, q, c). `k_diag`: every block is symmetric with diagonal entries of 1 or more. `m_diag`: every block is symmetric with diagonal entries of 1 or more.
All inputs are finite; a program needn't handle non-finite values.
Results may differ from the reference program's by a relative error of at most 0.0003.
Values sent between devices are 32-bit elements; how exact they have to be, the bound alone decides.
No kernel may reach another device: no remote copies, remote signals or barrier semaphores. Data moves between devices by JAX's collectives and lax.ppermute only.
A program may use at most 128 MiB of HBM per device.

```python
import math
import jax
import jax.numpy as jnp
from jax import lax

MODES = 96
SN = 64
NS = 8
NBL = 4
CAP = 3
STEPS = 2
RR_ITERS = 3
OWNERS = 64
SLOTS = 192
NODES = 512
DOF = 32768


def coupling_scale():
    return 0.3 / math.sqrt(SN * (2 * NBL + (SLOTS + NS - 1) // NS + 1))


def diagonal_entries(key, upper):
    first, second = jax.random.split(key)
    noise = jax.random.uniform(first, (NODES, SN, SN), jnp.float32, -1.0, 1.0) * coupling_scale()
    noise = 0.5 * (noise + jnp.swapaxes(noise, 1, 2))
    values = jnp.exp(jax.random.uniform(second, (NODES, SN), jnp.float32, 0.0, math.log(upper)))
    ident = jnp.eye(SN, dtype=jnp.float32)
    return (noise * (1.0 - ident) + values[:, :, None] * ident).astype(jnp.bfloat16)


def draw_k_diag(key, part):
    return diagonal_entries(key, 10.0)


def draw_m_diag(key, part):
    return diagonal_entries(jax.random.fold_in(key, 7), 3.0)


def link_entries(key):
    return (jax.random.uniform(key, (NODES, NBL, SN, SN), jnp.float32, -1.0, 1.0) * coupling_scale()).astype(jnp.bfloat16)


def draw_k_link(key, part):
    return link_entries(jax.random.fold_in(key, 11))


def draw_m_link(key, part):
    return link_entries(jax.random.fold_in(key, 13))


def interface_entries(key):
    entries = jax.random.uniform(key, (OWNERS, OWNERS, CAP, SN, SN), jnp.float32, -1.0, 1.0) * coupling_scale()
    flipped = jnp.transpose(entries, (1, 0, 2, 4, 3))
    first_owner = jnp.arange(OWNERS, dtype=jnp.int32)[:, None, None, None, None]
    second_owner = jnp.arange(OWNERS, dtype=jnp.int32)[None, :, None, None, None]
    return jnp.where(first_owner < second_owner, entries, flipped).astype(jnp.bfloat16)


def draw_k_iface(key, part):
    return interface_entries(jax.random.fold_in(key, 17))


def draw_m_iface(key, part):
    return interface_entries(jax.random.fold_in(key, 19))


def slot_permutation(single_key):
    return jax.random.permutation(single_key, SLOTS)


def supernode_permutation(single_key):
    return jax.random.permutation(single_key, NS)


def draw_iface_local(key, part):
    keys = jax.random.split(jax.random.fold_in(key, 23), OWNERS)
    perms = jax.vmap(slot_permutation)(keys)
    return (perms % NS).reshape(OWNERS, OWNERS, CAP).astype(jnp.int32)


def draw_iface_live(key, part):
    first, second = jax.random.split(jax.random.fold_in(key, 29))
    weights = jax.random.randint(first, (OWNERS,), 4, 48)
    score = jax.random.randint(second, (OWNERS, OWNERS, CAP), 0, 100)
    score_flip = jnp.transpose(score, (1, 0, 2))
    first_owner = jnp.arange(OWNERS, dtype=jnp.int32)[:, None, None]
    second_owner = jnp.arange(OWNERS, dtype=jnp.int32)[None, :, None]
    paired = jnp.where(first_owner < second_owner, score, score_flip)
    live = (paired < weights[:, None, None] + weights[None, :, None]) & (first_owner != second_owner)
    return live.astype(jnp.int32)


def draw_link_to(key, part):
    keys = jax.random.split(jax.random.fold_in(key, 31), OWNERS * NBL)
    perms = jax.vmap(supernode_permutation)(keys).reshape(OWNERS, NBL, NS)
    return jnp.transpose(perms, (0, 2, 1)).reshape(NODES, NBL).astype(jnp.int32)


def draw_link_count(key, part):
    counts = jax.random.randint(jax.random.fold_in(key, 37), (NODES,), 1, NBL + 1)
    first_node = jnp.arange(NODES, dtype=jnp.int32) % NS == 0
    return jnp.where(first_node, NBL, counts).astype(jnp.int32)


def level_of(stream_key, extent, cuts, least, high):
    level = 1.0
    for position, parts in cuts:
        steps = jax.random.uniform(jax.random.fold_in(jax.random.fold_in(stream_key, 6), position), (parts,), jnp.float32, least / len(cuts), high / len(cuts))
        level = level * jnp.repeat(jnp.exp(steps), extent[position] // parts).reshape((-1,) + (1,) * (len(extent) - 1 - position))
    return level


def bell_draw(rng, shape, width, limit, cuts=(), held_as=jnp.bfloat16):
    values = width * jax.random.normal(rng, shape, jnp.float32)
    if cuts:
        values = values * level_of(rng, shape, cuts, -0.22, 0.18)
    return jnp.clip(values, -limit, limit).astype(held_as)


def setup_inputs(seed: int = 0) -> dict:
    splits = jax.random.split(jax.random.key(seed), 13)
    x_start = bell_draw(splits[0], (MODES, DOF), 1.0, 6.0, ((0, 8), (1, 64)), jnp.float32)
    p_start = bell_draw(splits[1], (MODES, DOF), 1.0, 6.0, ((0, 8), (1, 64)), jnp.float32)
    k_diag = draw_k_diag(jax.random.fold_in(splits[12], 71), 0)
    k_link = draw_k_link(jax.random.fold_in(splits[12], 71), 0)
    m_diag = draw_m_diag(jax.random.fold_in(splits[12], 71), 0)
    m_link = draw_m_link(jax.random.fold_in(splits[12], 71), 0)
    link_to = draw_link_to(jax.random.fold_in(splits[12], 71), 0)
    link_count = draw_link_count(jax.random.fold_in(splits[12], 71), 0)
    k_iface = draw_k_iface(jax.random.fold_in(splits[12], 71), 0)
    m_iface = draw_m_iface(jax.random.fold_in(splits[12], 71), 0)
    iface_local = draw_iface_local(jax.random.fold_in(splits[12], 71), 0)
    iface_live = draw_iface_live(jax.random.fold_in(splits[12], 71), 0)
    return {"x_start": x_start, "p_start": p_start, "k_diag": k_diag, "k_link": k_link, "m_diag": m_diag, "m_link": m_link, "link_to": link_to, "link_count": link_count, "k_iface": k_iface, "m_iface": m_iface, "iface_local": iface_local, "iface_live": iface_live}


exact_dots = lax.Precision.HIGHEST

def symmetric(matrix):
    return 0.5 * (matrix + matrix.T)

def local_product(vectors, diag_blocks, link_blocks, link_onehot, link_live):
    near = jnp.einsum('sbt,ctj->csbj', link_onehot, vectors, precision=exact_dots) * link_live[None, :, :, None]
    result = jnp.einsum('sij,csj->csi', diag_blocks.astype(jnp.float32), vectors, precision=exact_dots)
    result = result + jnp.einsum('sbij,csbj->csi', link_blocks.astype(jnp.float32), near, precision=exact_dots)
    back = jnp.einsum('sbji,csj->csbi', link_blocks.astype(jnp.float32), vectors, precision=exact_dots) * link_live[None, :, :, None]
    return result + jnp.einsum('sbt,csbi->cti', link_onehot, back, precision=exact_dots)

def apply_pair(vectors, k_diag, k_link, m_diag, m_link, link_to, link_count, k_iface, m_iface, iface_local, iface_live):
    col_count = vectors.shape[0]
    owners = k_iface.shape[0]
    node_size = k_diag.shape[1]
    node_count = k_diag.shape[0] // owners
    link_slots = link_to.shape[1]
    split_vec = jnp.transpose(vectors.reshape(col_count, owners, node_count, node_size), (1, 0, 2, 3))
    link_onehot = (link_to[:, :, None] == jnp.arange(node_count, dtype=jnp.int32)[None, None, :]).astype(jnp.float32)
    link_live = (jnp.arange(link_slots, dtype=jnp.int32)[None, :] < link_count[:, None]).astype(jnp.float32)

    def by_owner(array):
        return array.reshape((owners, node_count) + array.shape[1:])

    def one_owner(pieces):
        vecs, stiff_d, stiff_l, mass_d, mass_l, onehot, live = pieces
        return (local_product(vecs, stiff_d, stiff_l, onehot, live), local_product(vecs, mass_d, mass_l, onehot, live))
    stiff, mass = lax.map(one_owner, (split_vec, by_owner(k_diag), by_owner(k_link), by_owner(m_diag), by_owner(m_link), by_owner(link_onehot), by_owner(link_live)))
    slot_onehot = (iface_local[:, :, :, None] == jnp.arange(node_count, dtype=jnp.int32)).astype(jnp.float32)
    slot_live = iface_live.astype(jnp.float32)
    recv_onehot = jnp.transpose(slot_onehot, (1, 0, 2, 3))

    def sender(totals, pieces):
        vecs, stiff_f, mass_f, send_onehot, live_send, arrive_onehot = pieces
        picked = jnp.einsum('qas,csj->qacj', send_onehot, vecs, precision=exact_dots)
        part_k = jnp.einsum('qaij,qacj->qaci', stiff_f.astype(jnp.float32), picked, precision=exact_dots) * live_send[:, :, None, None]
        part_m = jnp.einsum('qaij,qacj->qaci', mass_f.astype(jnp.float32), picked, precision=exact_dots) * live_send[:, :, None, None]
        add_k = jnp.einsum('qas,qaci->qcsi', arrive_onehot, part_k, precision=exact_dots)
        add_m = jnp.einsum('qas,qaci->qcsi', arrive_onehot, part_m, precision=exact_dots)
        return ((totals[0] + add_k, totals[1] + add_m), None)
    zeros = jnp.zeros(stiff.shape, jnp.float32)
    (face_k, face_m), unused = lax.scan(sender, (zeros, zeros), (split_vec, k_iface, m_iface, slot_onehot, slot_live, recv_onehot))
    stiff = jnp.transpose(stiff + face_k, (1, 0, 2, 3)).reshape(col_count, -1)
    mass = jnp.transpose(mass + face_m, (1, 0, 2, 3)).reshape(col_count, -1)
    return (stiff, mass)

def rayleigh(gram_stiff, gram_mass, modes):
    total = gram_stiff.shape[0]
    factor = jnp.linalg.cholesky(gram_stiff)
    coeffs = jnp.eye(total, modes, dtype=jnp.float32)
    for inner_index in range(RR_ITERS):
        solved = jax.scipy.linalg.cho_solve((factor, True), jnp.dot(gram_mass, coeffs, precision=exact_dots))
        inner = symmetric(jnp.dot(solved.T, jnp.dot(gram_mass, solved, precision=exact_dots), precision=exact_dots))
        inner_factor = jnp.linalg.cholesky(inner)
        coeffs = jax.scipy.linalg.solve_triangular(inner_factor, solved.T, lower=True).T
    ritz_new = symmetric(jnp.dot(coeffs.T, jnp.dot(gram_stiff, coeffs, precision=exact_dots), precision=exact_dots))
    return (coeffs, ritz_new)

def reference(x_start, p_start, k_diag, k_link, m_diag, m_link, link_to, link_count, k_iface, m_iface, iface_local, iface_live):
    modes, dof_count = x_start.shape
    tables = (k_diag, k_link, m_diag, m_link, link_to, link_count, k_iface, m_iface, iface_local, iface_live)
    both_k, both_m = apply_pair(jnp.concatenate([x_start, p_start], 0), *tables)
    stiff_x, stiff_p = (both_k[:modes], both_k[modes:])
    mass_x, mass_p = (both_m[:modes], both_m[modes:])
    precond = 1.0 / jnp.diagonal(k_diag.astype(jnp.float32), axis1=1, axis2=2).reshape(-1)
    x_block, p_block = (x_start, p_start)
    stiff_gram = symmetric(jnp.dot(x_block, stiff_x.T, precision=exact_dots) / dof_count)
    mass_gram = symmetric(jnp.dot(x_block, mass_x.T, precision=exact_dots) / dof_count)
    ritz_now = jax.scipy.linalg.cho_solve((jnp.linalg.cholesky(mass_gram), True), stiff_gram)
    for step_index in range(STEPS):
        resid = stiff_x - jnp.dot(ritz_now.T, mass_x, precision=exact_dots)
        search = resid * precond[None, :]
        stiff_w, mass_w = apply_pair(search, *tables)
        space = jnp.concatenate([x_block, search, p_block], 0)
        space_k = jnp.concatenate([stiff_x, stiff_w, stiff_p], 0)
        space_m = jnp.concatenate([mass_x, mass_w, mass_p], 0)
        gram_stiff = symmetric(jnp.dot(space, space_k.T, precision=exact_dots) / dof_count)
        gram_mass = symmetric(jnp.dot(space, space_m.T, precision=exact_dots) / dof_count)
        coeffs, ritz_new = rayleigh(gram_stiff, gram_mass, modes)
        x_block = jnp.dot(coeffs.T, space, precision=exact_dots)
        p_block = jnp.dot(coeffs[modes:].T, space[modes:], precision=exact_dots)
        if step_index + 1 < STEPS:
            stiff_x = jnp.dot(coeffs.T, space_k, precision=exact_dots)
            mass_x = jnp.dot(coeffs.T, space_m, precision=exact_dots)
            stiff_p = jnp.dot(coeffs[modes:].T, space_k[modes:], precision=exact_dots)
            mass_p = jnp.dot(coeffs[modes:].T, space_m[modes:], precision=exact_dots)
        ritz_now = ritz_new
    return (x_block, p_block, ritz_now)
```

```python
import jax
import jax.numpy as jnp
from jax import lax
from jax.sharding import PartitionSpec as P

STEPS = 2
RR_ITERS = 3


exact_dots = lax.Precision.HIGHEST


def symmetric(matrix):
    return 0.5 * (matrix + matrix.T)


def edot(a, b):
    return jnp.dot(a, b, precision=exact_dots)


def split_three(values):
    high = lax.reduce_precision(values, 8, 7)
    rest = values - high
    middle = lax.reduce_precision(rest, 8, 7)
    low = rest - middle
    return (high, middle, low)


def swap(array, axis):
    return lax.all_to_all(array, axis, split_axis=0, concat_axis=0, tiled=True)


def spread(array, axis):
    count = lax.axis_size(axis)
    return swap(jnp.broadcast_to(array[None], (count,) + array.shape), axis)


def exchange(vectors, slot_ids, node_count):
    col_count, row_count = vectors.shape
    by_node = jnp.transpose(vectors.reshape(col_count, node_count, -1), (1, 0, 2)).reshape(
        node_count, -1
    )
    picked = jnp.zeros((slot_ids.shape[0], by_node.shape[1]), jnp.float32)
    for node in range(node_count):
        picked = jnp.where(slot_ids[:, None] == node, by_node[node][None, :], picked)
    owners = lax.axis_size("rows")
    received = swap(picked.reshape(owners, -1), "rows")
    return received.reshape(slot_ids.shape[0], col_count, -1)


def apply_pair(vectors, received, tables):
    blocks, src_onehot, dst_onehot, node_count = tables
    col_count, row_count = vectors.shape
    by_node = jnp.transpose(vectors.reshape(col_count, node_count, -1), (1, 0, 2))
    near = jnp.einsum("ks,scj->kcj", src_onehot, by_node, precision=exact_dots)
    sources = jnp.concatenate([received, near], 0)
    stacked = jnp.concatenate(split_three(sources), 1).astype(jnp.bfloat16)
    products = jnp.einsum("kcj,kjn->kcn", stacked, blocks, preferred_element_type=jnp.float32)
    products = (
        products[:, :col_count]
        + products[:, col_count : 2 * col_count]
        + products[:, 2 * col_count :]
    )
    sums = jnp.einsum("ks,kcn->csn", dst_onehot, products, precision=exact_dots)
    half = sums.shape[2] // 2
    return (
        sums[:, :, :half].reshape(col_count, row_count),
        sums[:, :, half:].reshape(col_count, row_count),
    )


def reduce_gram(rows, own_k, own_m, dof_count):
    part = jnp.einsum(
        "nr,cr->nc", rows, jnp.concatenate([own_k, own_m], 0), precision=exact_dots
    )
    extent, width = part.shape
    owners = lax.axis_size("rows")
    summed = jnp.sum(swap(part.reshape(owners, -1), "rows"), 0)
    whole = spread(spread(summed, "rows").reshape(-1), "cols")
    col_count = own_k.shape[0]
    whole = whole.reshape(-1, extent, 2, col_count)
    whole = jnp.transpose(whole, (2, 1, 0, 3)).reshape(2, extent, -1) / dof_count
    return whole[0], whole[1]


def rayleigh(gram_stiff, gram_mass, modes):
    total = gram_stiff.shape[0]
    factor = jnp.linalg.cholesky(gram_stiff)
    coeffs = jnp.eye(total, modes, dtype=jnp.float32)
    for inner_index in range(RR_ITERS):
        solved = jax.scipy.linalg.cho_solve((factor, True), edot(gram_mass, coeffs))
        inner = symmetric(edot(solved.T, edot(gram_mass, solved)))
        inner_factor = jnp.linalg.cholesky(inner)
        coeffs = jax.scipy.linalg.solve_triangular(inner_factor, solved.T, lower=True).T
    ritz_new = symmetric(edot(coeffs.T, edot(gram_stiff, coeffs)))
    return (coeffs, ritz_new)


def assemble(xx, xp, pp, column):
    modes = xx.shape[0]
    xw = column[:modes]
    ww = symmetric(column[modes : 2 * modes])
    pw = column[2 * modes :]
    return jnp.concatenate(
        [
            jnp.concatenate([xx, xw, xp], 1),
            jnp.concatenate([xw.T, ww, pw.T], 1),
            jnp.concatenate([xp.T, pw, pp], 1),
        ],
        0,
    )


def body(
    x_start,
    p_start,
    k_diag,
    k_link,
    m_diag,
    m_link,
    link_to,
    link_count,
    k_iface,
    m_iface,
    iface_local,
    iface_live,
):
    col_part, row_count = x_start.shape
    modes = col_part * lax.axis_size("cols")
    dof_count = row_count * lax.axis_size("rows")
    node_count, link_slots = link_to.shape
    node_size = k_diag.shape[1]
    node_ids = jnp.arange(node_count, dtype=jnp.int32)
    slot_ids = iface_local.reshape(-1)
    slot_live = iface_live.reshape(-1) > 0
    link_live = jnp.arange(link_slots, dtype=jnp.int32)[None, :] < link_count[:, None]

    def side_by_side(k_part, m_part, live):
        pair = jnp.concatenate([k_part, m_part], 2)
        return jnp.where(live[:, None, None], pair, jnp.zeros_like(pair))

    def flat(blocks):
        return blocks.reshape(-1, node_size, node_size)

    def flipped(blocks):
        return jnp.swapaxes(flat(blocks), 1, 2)

    live_flat = link_live.reshape(-1)
    blocks = jnp.concatenate(
        [
            side_by_side(flat(k_iface), flat(m_iface), slot_live),
            side_by_side(k_diag, m_diag, jnp.ones((node_count,), bool)),
            side_by_side(flipped(k_link), flipped(m_link), live_flat),
            side_by_side(flat(k_link), flat(m_link), live_flat),
        ],
        0,
    )
    link_from = jnp.repeat(node_ids, link_slots)
    link_flat = link_to.reshape(-1)
    src_ids = jnp.concatenate([node_ids, link_flat, link_from])
    dst_ids = jnp.concatenate([slot_ids, node_ids, link_from, link_flat])
    src_onehot = (src_ids[:, None] == node_ids[None, :]).astype(jnp.float32)
    dst_onehot = (dst_ids[:, None] == node_ids[None, :]).astype(jnp.float32)
    tables = (blocks, src_onehot, dst_onehot, node_count)

    precond = 1.0 / jnp.diagonal(k_diag.astype(jnp.float32), axis1=1, axis2=2).reshape(-1)
    col_start = lax.axis_index("cols") * col_part

    received_x = exchange(x_start, slot_ids, node_count)
    both = spread(jnp.stack([x_start, p_start]), "cols")
    all_x = both[:, 0].reshape(modes, row_count)
    all_p = both[:, 1].reshape(modes, row_count)
    own_kx, own_mx = apply_pair(x_start, received_x, tables)
    stiff_xx, mass_xx = reduce_gram(all_x, own_kx, own_mx, dof_count)
    stiff_xx, mass_xx = symmetric(stiff_xx), symmetric(mass_xx)
    received_p = exchange(p_start, slot_ids, node_count)
    own_kp, own_mp = apply_pair(p_start, received_p, tables)
    moved = spread(jnp.stack([own_kx, own_mx, own_kp, own_mp]), "cols")
    all_kx, all_mx, all_kp, all_mp = [moved[:, i].reshape(modes, row_count) for i in range(4)]
    stiff_p, mass_p = reduce_gram(
        jnp.concatenate([all_x, all_p], 0), own_kp, own_mp, dof_count
    )
    stiff_xp, stiff_pp = stiff_p[:modes], symmetric(stiff_p[modes:])
    mass_xp, mass_pp = mass_p[:modes], symmetric(mass_p[modes:])

    ritz_now = jax.scipy.linalg.cho_solve((jnp.linalg.cholesky(mass_xx), True), stiff_xx)
    for step_index in range(STEPS):
        all_w = (all_kx - edot(ritz_now.T, all_mx)) * precond[None, :]
        own_w = lax.dynamic_slice_in_dim(all_w, col_start, col_part, 0)
        received_w = exchange(own_w, slot_ids, node_count)
        own_kw, own_mw = apply_pair(own_w, received_w, tables)
        space = jnp.concatenate([all_x, all_w, all_p], 0)
        stiff_w, mass_w = reduce_gram(space, own_kw, own_mw, dof_count)
        gram_stiff = assemble(stiff_xx, stiff_xp, stiff_pp, stiff_w)
        gram_mass = assemble(mass_xx, mass_xp, mass_pp, mass_w)
        coeffs, ritz_now = rayleigh(gram_stiff, gram_mass, modes)
        if step_index + 1 == STEPS:
            mine = lax.dynamic_slice_in_dim(coeffs, col_start, col_part, 1)
            p_out = edot(mine[modes:].T, space[modes:])
            x_out = p_out + edot(mine[:modes].T, space[:modes])
            return (x_out, p_out, ritz_now)
        moved = spread(jnp.stack([own_kw, own_mw]), "cols")
        all_kw, all_mw = [moved[:, i].reshape(modes, row_count) for i in range(2)]
        wide = jnp.concatenate(
            [
                space,
                jnp.concatenate([all_kx, all_kw, all_kp], 0),
                jnp.concatenate([all_mx, all_mw, all_mp], 0),
            ],
            1,
        )
        new_p = edot(coeffs[modes:].T, wide[modes:])
        new_x = new_p + edot(coeffs[:modes].T, wide[:modes])
        all_x, all_kx, all_mx = [new_x[:, i * row_count : (i + 1) * row_count] for i in range(3)]
        all_p, all_kp, all_mp = [new_p[:, i * row_count : (i + 1) * row_count] for i in range(3)]
        tail = coeffs.at[:modes].set(0.0)
        pair = jnp.concatenate([coeffs, tail], 1)
        next_stiff = symmetric(edot(pair.T, edot(gram_stiff, pair)))
        next_mass = symmetric(edot(pair.T, edot(gram_mass, pair)))
        stiff_xx, stiff_xp, stiff_pp = (
            next_stiff[:modes, :modes],
            next_stiff[:modes, modes:],
            next_stiff[modes:, modes:],
        )
        mass_xx, mass_xp, mass_pp = (
            next_mass[:modes, :modes],
            next_mass[:modes, modes:],
            next_mass[modes:, modes:],
        )


def solution(mesh):
    placed = (
        P("cols", "rows"),
        P("cols", "rows"),
        P("rows", None, None),
        P("rows", None, None, None),
        P("rows", None, None),
        P("rows", None, None, None),
        P("rows", None),
        P("rows"),
        P("rows", None, None, None, None),
        P("rows", None, None, None, None),
        P("rows", None, None),
        P("rows", None, None),
    )
    return jax.shard_map(
        body,
        mesh=mesh,
        in_specs=placed,
        out_specs=(P("cols", "rows"), P("cols", "rows"), P()),
        check_vma=False,
    )
```

```python
import jax
import jax.numpy as jnp
from jax import lax
from jax.experimental import pallas as pl
from jax.experimental.pallas import tpu as pltpu
from jax.sharding import PartitionSpec as P

STEPS = 2
RR_ITERS = 3


exact_dots = lax.Precision.HIGHEST


def edot(a, b):
    return jnp.dot(a, b, precision=exact_dots)


def split_three(values):
    high = lax.reduce_precision(values, 8, 7)
    rest = values - high
    middle = lax.reduce_precision(rest, 8, 7)
    low = rest - middle
    return (high, middle, low)


def swap(array, axis):
    return lax.all_to_all(array, axis, split_axis=0, concat_axis=0, tiled=True)


def spread(array, axis):
    count = lax.axis_size(axis)
    return swap(jnp.broadcast_to(array[None], (count,) + array.shape), axis)


def exchange(vectors, slot_ids, node_count):
    col_count, row_count = vectors.shape
    by_node = jnp.transpose(vectors.reshape(col_count, node_count, -1), (1, 0, 2)).reshape(
        node_count, -1
    )
    picked = jnp.zeros((slot_ids.shape[0], by_node.shape[1]), jnp.float32)
    for node in range(node_count):
        picked = jnp.where(slot_ids[:, None] == node, by_node[node][None, :], picked)
    owners = lax.axis_size("rows")
    received = swap(picked.reshape(owners, -1), "rows")
    return received.reshape(slot_ids.shape[0], col_count, -1)


def apply_pair(vectors, received, tables):
    blocks, src_onehot, dst_onehot, node_count = tables
    col_count, row_count = vectors.shape
    by_node = jnp.transpose(vectors.reshape(col_count, node_count, -1), (1, 0, 2))
    near = jnp.einsum("ks,scj->kcj", src_onehot, by_node, precision=exact_dots)
    sources = jnp.concatenate([received, near], 0)
    stacked = jnp.concatenate(split_three(sources), 1).astype(jnp.bfloat16)
    products = jnp.einsum("kcj,kjn->kcn", stacked, blocks, preferred_element_type=jnp.float32)
    products = (
        products[:, :col_count]
        + products[:, col_count : 2 * col_count]
        + products[:, 2 * col_count :]
    )
    sums = jnp.einsum("ks,kcn->csn", dst_onehot, products, precision=exact_dots)
    half = sums.shape[2] // 2
    return (
        sums[:, :, :half].reshape(col_count, row_count),
        sums[:, :, half:].reshape(col_count, row_count),
    )


def reduce_gram(rows, own_k, own_m, dof_count):
    own = jnp.concatenate([own_k, own_m], 0)
    part = jnp.einsum("cr,nr->cn", own, rows, precision=exact_dots) / dof_count
    owners = lax.axis_size("rows")
    summed = jnp.sum(swap(part.reshape(owners, -1), "rows"), 0)
    whole = spread(spread(summed, "rows").reshape(-1), "cols")
    whole = whole.reshape(-1, 2, own_k.shape[0], rows.shape[0])
    return [whole[:, i].reshape(-1, rows.shape[0]) for i in range(2)]


def nn(a, b):
    return lax.dot_general(
        a, b, (((1,), (0,)), ((), ())), precision=exact_dots, preferred_element_type=jnp.float32
    )


def nt(a, b):
    return lax.dot_general(
        a, b, (((1,), (1,)), ((), ())), precision=exact_dots, preferred_element_type=jnp.float32
    )


LANES = 128
PANEL = 8

def lower_inverse(matrix, out_ref):
    size = matrix.shape[0]
    tiles = size // PANEL
    wide = jnp.concatenate([matrix, jnp.zeros((size, LANES - size), jnp.float32)], 1)
    row = lax.broadcasted_iota(jnp.int32, (size, LANES), 0)
    lane = lax.broadcasted_iota(jnp.int32, (size, LANES), 1)
    ident = jnp.where(row == lane, 1.0, 0.0).astype(jnp.float32)
    left = [wide[PANEL * t : PANEL * t + PANEL] for t in range(tiles)]
    right = [ident[PANEL * t : PANEL * t + PANEL] for t in range(tiles)]
    full = (PANEL, LANES)

    def lane_splat(tile, k):
        return jnp.broadcast_to(tile[:, k : k + 1], full)

    def row_splat(tile, i):
        return jnp.broadcast_to(tile[i : i + 1, :], full)

    for p in range(tiles):
        base = PANEL * p
        cols = [lane_splat(left[p], base + k) for k in range(PANEL)]
        s = {(i, k): row_splat(cols[k], i) for k in range(PANEL) for i in range(k, PANEL)}
        low = {}
        inv = {}
        for k in range(PANEL):
            d = s[k, k]
            r = lax.rsqrt(d)
            r = r * (1.5 - 0.5 * d * r * r)
            inv[k, k] = r
            for i in range(k + 1, PANEL):
                low[i, k] = s[i, k] * r
            for m in range(k + 1, PANEL):
                for i in range(m, PANEL):
                    s[i, m] = s[i, m] - low[i, k] * low[m, k]
        for i in range(1, PANEL):
            for j in range(i):
                acc = low[i, j] * inv[j, j]
                for k in range(j + 1, i):
                    acc = acc + low[i, k] * inv[k, j]
                inv[i, j] = -inv[i, i] * acc
        rows_l = [row_splat(left[p], i) for i in range(PANEL)]
        rows_r = [row_splat(right[p], i) for i in range(PANEL)]
        new_l, new_r = [], []
        for i in range(PANEL):
            al = inv[i, 0] * rows_l[0]
            ar = inv[i, 0] * rows_r[0]
            for k in range(1, i + 1):
                al = al + inv[i, k] * rows_l[k]
                ar = ar + inv[i, k] * rows_r[k]
            new_l.append(al)
            new_r.append(ar)
            out_ref[base + i : base + i + 1, :] = ar[0:1, :size]
        for t in range(p + 1, tiles):
            ct = [lane_splat(left[t], base + k) for k in range(PANEL)]
            for k in range(PANEL):
                f = inv[k, 0] * ct[0]
                for j in range(1, k + 1):
                    f = f + inv[k, j] * ct[j]
                left[t] = left[t] - f * new_l[k]
                right[t] = right[t] - f * new_r[k]


def first_ritz_kernel(stiff_ref, mass_ref, ritz_ref, tmp_ref):
    lower_inverse(mass_ref[...], tmp_ref)
    inv = tmp_ref[...]
    ritz_ref[...] = nn(nt(stiff_ref[...], inv), inv)


def factor_old(stiff, mass, j_ref, jm_ref, b_ref, tmp_ref):
    n = tmp_ref.shape[0]
    lower_inverse(stiff[:n, :n], tmp_ref)
    first = tmp_ref[...]
    q = nt(stiff[n:, :n], first)
    lower_inverse(stiff[n:, n:] - nt(q, q), tmp_ref)
    second = tmp_ref[...]
    j_ref[:n, :n] = first
    j_ref[:n, n:] = jnp.zeros((n, n), jnp.float32)
    j_ref[n:, :n] = -nn(second, nn(q, first))
    j_ref[n:, n:] = second
    j = j_ref[...]
    jm = nt(mass, j)
    jm_ref[...] = jm
    b_ref[...] = nn(j, jm)


def old_kernel(stiff_ref, mass_ref, j_ref, jm_ref, b_ref, tmp_ref):
    factor_old(stiff_ref[...], mass_ref[...], j_ref, jm_ref, b_ref, tmp_ref)


def carry_kernel(
    y_ref, gxp_ref, mxp_ref, gw_ref, mw_ref, next_ref, j_ref, jm_ref, b_ref, tmp_ref
):
    n = tmp_ref.shape[0]
    ya = y_ref[:, : 2 * n]
    yb = y_ref[:, 2 * n :]
    lane = lax.broadcasted_iota(jnp.int32, ya.shape, 1)
    pa = jnp.concatenate([ya, jnp.where(lane < n, 0.0, ya)], 0)
    pb = jnp.concatenate([yb, yb], 0)

    def turned(old_ref, col_ref):
        col = col_ref[:, : 2 * n]
        ha = nn(pa, old_ref[...]) + nn(pb, col)
        hb = nt(pa, col) + nn(pb, col_ref[:, 2 * n :])
        return nt(ha, pa) + nt(hb, pb)

    mass = turned(mxp_ref, mw_ref)
    next_ref[...] = mass
    factor_old(turned(gxp_ref, gw_ref), mass, j_ref, jm_ref, b_ref, tmp_ref)


def ritz_kernel(
    gw_ref, mw_ref, mxp_ref, j_ref, jm_ref, b_ref, y_ref, ritz_ref, tmp_ref
):
    n = tmp_ref.shape[0]
    j = j_ref[...]
    bxx = b_ref[...]
    qt = nt(gw_ref[:, : 2 * n], j)
    lower_inverse(gw_ref[:, 2 * n :] - nt(qt, qt), tmp_ref)
    lw = tmp_ref[...]
    t = nn(qt, j)
    mwx = mw_ref[:, : 2 * n]
    d = mwx - nn(t, mxp_ref[...])
    e = mw_ref[:, 2 * n :] - nt(t, mwx) - nt(d, t)
    bwx = nn(lw, nt(d, j))
    bww = nt(nn(lw, e), lw)
    va = jm_ref[:n, :]
    vb = jnp.transpose(nn(lw, d[:, :n]))
    ua = ub = None
    for inner_index in range(RR_ITERS):
        wa = nn(va, bxx) + nn(vb, bwx)
        wb = nt(va, bwx) + nn(vb, bww)
        lower_inverse(nt(wa, va) + nt(wb, vb), tmp_ref)
        lc = tmp_ref[...]
        ua, ub = nn(lc, va), nn(lc, vb)
        va, vb = nn(lc, wa), nn(lc, wb)
    ritz_ref[...] = nt(ua, ua) + nt(ub, ub)
    yw = nn(ub, lw)
    y_ref[:, : 2 * n] = nn(ua, j) - nn(yw, t)
    y_ref[:, 2 * n :] = yw


def dense(kernel, shapes, size):
    return pl.pallas_call(
        kernel,
        out_shape=tuple(jax.ShapeDtypeStruct(s, jnp.float32) for s in shapes),
        scratch_shapes=[pltpu.VMEM((size, size), jnp.float32)],
    )


def body(
    x_start,
    p_start,
    k_diag,
    k_link,
    m_diag,
    m_link,
    link_to,
    link_count,
    k_iface,
    m_iface,
    iface_local,
    iface_live,
):
    col_part, row_count = x_start.shape
    modes = col_part * lax.axis_size("cols")
    dof_count = row_count * lax.axis_size("rows")
    node_count, link_slots = link_to.shape
    node_size = k_diag.shape[1]
    node_ids = jnp.arange(node_count, dtype=jnp.int32)
    slot_ids = iface_local.reshape(-1)
    slot_live = iface_live.reshape(-1) > 0
    link_live = jnp.arange(link_slots, dtype=jnp.int32)[None, :] < link_count[:, None]

    def side_by_side(k_part, m_part, live):
        pair = jnp.concatenate([k_part, m_part], 2)
        return jnp.where(live[:, None, None], pair, jnp.zeros_like(pair))

    def flat(blocks):
        return blocks.reshape(-1, node_size, node_size)

    def flipped(blocks):
        return jnp.swapaxes(flat(blocks), 1, 2)

    live_flat = link_live.reshape(-1)
    blocks = jnp.concatenate(
        [
            side_by_side(flat(k_iface), flat(m_iface), slot_live),
            side_by_side(k_diag, m_diag, jnp.ones((node_count,), bool)),
            side_by_side(flipped(k_link), flipped(m_link), live_flat),
            side_by_side(flat(k_link), flat(m_link), live_flat),
        ],
        0,
    )
    link_from = jnp.repeat(node_ids, link_slots)
    link_flat = link_to.reshape(-1)
    src_ids = jnp.concatenate([node_ids, link_flat, link_from])
    dst_ids = jnp.concatenate([slot_ids, node_ids, link_from, link_flat])
    src_onehot = (src_ids[:, None] == node_ids[None, :]).astype(jnp.float32)
    dst_onehot = (dst_ids[:, None] == node_ids[None, :]).astype(jnp.float32)
    tables = (blocks, src_onehot, dst_onehot, node_count)

    precond = 1.0 / jnp.diagonal(k_diag.astype(jnp.float32), axis1=1, axis2=2).reshape(-1)
    col_start = lax.axis_index("cols") * col_part

    both = spread(jnp.stack([x_start, p_start]), "cols")
    received_x = exchange(x_start, slot_ids, node_count)
    received_p = exchange(p_start, slot_ids, node_count)
    all_x = both[:, 0].reshape(modes, row_count)
    all_p = both[:, 1].reshape(modes, row_count)
    own_kx, own_mx = apply_pair(x_start, received_x, tables)
    stiff_xx, mass_xx = reduce_gram(all_x, own_kx, own_mx, dof_count)
    moved = spread(jnp.stack([own_kx, own_mx]), "cols")
    all_kx, all_mx = [moved[:, i].reshape(modes, row_count) for i in range(2)]
    own_kp, own_mp = apply_pair(p_start, received_p, tables)
    stiff_p, mass_p = reduce_gram(
        jnp.concatenate([all_x, all_p], 0), own_kp, own_mp, dof_count
    )

    def old_block(xx, column):
        return jnp.concatenate(
            [jnp.concatenate([xx, column[:, :modes].T], 1), column], 0
        )

    square = (modes, modes)
    pair = (2 * modes, 2 * modes)
    old_stiff, old_mass = old_block(stiff_xx, stiff_p), old_block(mass_xx, mass_p)
    factors = dense(old_kernel, (pair,) * 3, modes)(old_stiff, old_mass)
    (ritz_turned,) = dense(first_ritz_kernel, (square,), modes)(stiff_xx, mass_xx)
    for step_index in range(STEPS):
        all_w = (all_kx - edot(ritz_turned, all_mx)) * precond[None, :]
        own_w = lax.dynamic_slice_in_dim(all_w, col_start, col_part, 0)
        received_w = exchange(own_w, slot_ids, node_count)
        own_kw, own_mw = apply_pair(own_w, received_w, tables)
        space = jnp.concatenate([all_x, all_p, all_w], 0)
        stiff_w, mass_w = reduce_gram(space, own_kw, own_mw, dof_count)
        coeffs, ritz_turned = dense(ritz_kernel, ((modes, 3 * modes), square), modes)(
            stiff_w, mass_w, old_mass, *factors
        )
        if step_index + 1 == STEPS:
            mine = lax.dynamic_slice_in_dim(coeffs, col_start, col_part, 0)
            p_out = edot(mine[:, modes:], space[modes:])
            x_out = p_out + edot(mine[:, :modes], space[:modes])
            return (x_out, p_out, ritz_turned)
        moved = spread(jnp.stack([own_kp, own_mp, own_kw, own_mw]), "cols")
        all_kp, all_mp, all_kw, all_mw = [
            moved[:, i].reshape(modes, row_count) for i in range(4)
        ]
        wide_x = jnp.concatenate([all_x, all_kx, all_mx], 1)
        wide_rest = jnp.concatenate(
            [
                jnp.concatenate([all_p, all_kp, all_mp], 1),
                jnp.concatenate([all_w, all_kw, all_mw], 1),
            ],
            0,
        )
        new_p = edot(coeffs[:, modes:], wide_rest)
        new_x = new_p + edot(coeffs[:, :modes], wide_x)
        all_x, all_kx, all_mx = [new_x[:, i * row_count : (i + 1) * row_count] for i in range(3)]
        all_p = new_p[:, :row_count]
        old_mass, *factors = dense(carry_kernel, (pair,) * 4, modes)(
            coeffs, old_stiff, old_mass, stiff_w, mass_w
        )


def solution(mesh):
    placed = (
        P("cols", "rows"),
        P("cols", "rows"),
        P("rows", None, None),
        P("rows", None, None, None),
        P("rows", None, None),
        P("rows", None, None, None),
        P("rows", None),
        P("rows"),
        P("rows", None, None, None, None),
        P("rows", None, None, None, None),
        P("rows", None, None),
        P("rows", None, None),
    )
    return jax.shard_map(
        body,
        mesh=mesh,
        in_specs=placed,
        out_specs=(P("cols", "rows"), P("cols", "rows"), P()),
        check_vma=False,
    )
```

```python
import jax
import jax.numpy as jnp
from jax import lax
from jax.experimental import pallas as pl
from jax.experimental.pallas import tpu as pltpu
from jax.sharding import Mesh, PartitionSpec as P

ROWS = ("z", "y")
COLS = ("x", "core")
Y_SIZE = 4
CORES = 2
STEPS = 2
RR_ITERS = 3


exact_dots = lax.Precision.HIGHEST


def edot(a, b):
    return jnp.dot(a, b, precision=exact_dots)


def split_three(values):
    high = lax.reduce_precision(values, 8, 7)
    rest = values - high
    middle = lax.reduce_precision(rest, 8, 7)
    low = rest - middle
    return (high, middle, low)


def swap(array, axis):
    return lax.all_to_all(array, axis, split_axis=0, concat_axis=0, tiled=True)


def spread(array, axis):
    count = lax.axis_size(axis)
    return swap(jnp.broadcast_to(array[None], (count,) + array.shape), axis)


def exchange(vectors, slot_ids, node_count):
    col_count, row_count = vectors.shape
    by_node = jnp.transpose(vectors.reshape(col_count, node_count, -1), (1, 0, 2)).reshape(
        node_count, -1
    )
    picked = jnp.zeros((slot_ids.shape[0], by_node.shape[1]), jnp.float32)
    for node in range(node_count):
        picked = jnp.where(slot_ids[:, None] == node, by_node[node][None, :], picked)
    owners = lax.axis_size(ROWS)
    received = swap(picked.reshape(owners, -1), ROWS)
    return received.reshape(slot_ids.shape[0], col_count, -1)


def apply_pair(vectors, received, tables):
    blocks, src_onehot, dst_onehot, node_count = tables
    col_count, row_count = vectors.shape
    by_node = jnp.transpose(vectors.reshape(col_count, node_count, -1), (1, 0, 2))
    near = jnp.einsum("ks,scj->kcj", src_onehot, by_node, precision=exact_dots)
    sources = jnp.concatenate([received, near], 0)
    stacked = jnp.concatenate(split_three(sources), 1).astype(jnp.bfloat16)
    products = jnp.einsum("kcj,kjn->kcn", stacked, blocks, preferred_element_type=jnp.float32)
    products = (
        products[:, :col_count]
        + products[:, col_count : 2 * col_count]
        + products[:, 2 * col_count :]
    )
    sums = jnp.einsum("ks,kcn->csn", dst_onehot, products, precision=exact_dots)
    half = sums.shape[2] // 2
    return (
        sums[:, :, :half].reshape(col_count, row_count),
        sums[:, :, half:].reshape(col_count, row_count),
    )


def gather_cols(*blocks):
    count = blocks[0].shape[0]
    moved = lax.all_gather(jnp.concatenate(blocks, 0), COLS, axis=0)
    return [
        moved[:, i * count : (i + 1) * count].reshape(-1, blocks[0].shape[1])
        for i in range(len(blocks))
    ]


def reduce_gram(rows, own, dof_count):
    part = jnp.einsum("cr,nr->cn", own, rows, precision=exact_dots) / dof_count
    piece = jnp.sum(swap(part.reshape(lax.axis_size("y"), -1), "y"), 0)
    piece = jnp.sum(spread(piece, "z"), 0)
    whole = spread(piece, ("y",) + COLS)
    whole = whole.reshape(lax.axis_size("y"), lax.axis_size(COLS), -1, rows.shape[0])
    return jnp.swapaxes(whole, 0, 1).reshape(lax.axis_size(COLS), own.shape[0], rows.shape[0])


def nn(a, b):
    return lax.dot_general(
        a, b, (((1,), (0,)), ((), ())), precision=exact_dots, preferred_element_type=jnp.float32
    )


def nt(a, b):
    return lax.dot_general(
        a, b, (((1,), (1,)), ((), ())), precision=exact_dots, preferred_element_type=jnp.float32
    )


LANES = 128
PANEL = 8

def lower_inverse(matrix, out_ref):
    size = matrix.shape[0]
    tiles = size // PANEL
    wide = jnp.concatenate([matrix, jnp.zeros((size, LANES - size), jnp.float32)], 1)
    row = lax.broadcasted_iota(jnp.int32, (size, LANES), 0)
    lane = lax.broadcasted_iota(jnp.int32, (size, LANES), 1)
    ident = jnp.where(row == lane, 1.0, 0.0).astype(jnp.float32)
    left = [wide[PANEL * t : PANEL * t + PANEL] for t in range(tiles)]
    right = [ident[PANEL * t : PANEL * t + PANEL] for t in range(tiles)]
    full = (PANEL, LANES)

    def lane_splat(tile, k):
        return jnp.broadcast_to(tile[:, k : k + 1], full)

    def row_splat(tile, i):
        return jnp.broadcast_to(tile[i : i + 1, :], full)

    for p in range(tiles):
        base = PANEL * p
        cols = [lane_splat(left[p], base + k) for k in range(PANEL)]
        s = {(i, k): row_splat(cols[k], i) for k in range(PANEL) for i in range(k, PANEL)}
        low = {}
        inv = {}
        for k in range(PANEL):
            d = s[k, k]
            r = lax.rsqrt(d)
            r = r * (1.5 - 0.5 * d * r * r)
            inv[k, k] = r
            for i in range(k + 1, PANEL):
                low[i, k] = s[i, k] * r
            for m in range(k + 1, PANEL):
                for i in range(m, PANEL):
                    s[i, m] = s[i, m] - low[i, k] * low[m, k]
        for i in range(1, PANEL):
            for j in range(i):
                acc = low[i, j] * inv[j, j]
                for k in range(j + 1, i):
                    acc = acc + low[i, k] * inv[k, j]
                inv[i, j] = -inv[i, i] * acc
        rows_l = [row_splat(left[p], i) for i in range(PANEL)]
        rows_r = [row_splat(right[p], i) for i in range(PANEL)]
        new_l, new_r = [], []
        for i in range(PANEL):
            al = inv[i, 0] * rows_l[0]
            ar = inv[i, 0] * rows_r[0]
            for k in range(1, i + 1):
                al = al + inv[i, k] * rows_l[k]
                ar = ar + inv[i, k] * rows_r[k]
            new_l.append(al)
            new_r.append(ar)
            out_ref[base + i : base + i + 1, :] = ar[0:1, :size]
        for t in range(p + 1, tiles):
            ct = [lane_splat(left[t], base + k) for k in range(PANEL)]
            for k in range(PANEL):
                f = inv[k, 0] * ct[0]
                for j in range(1, k + 1):
                    f = f + inv[k, j] * ct[j]
                left[t] = left[t] - f * new_l[k]
                right[t] = right[t] - f * new_r[k]


def first_ritz_kernel(stiff_ref, mass_ref, ritz_ref, tmp_ref):
    lower_inverse(mass_ref[...], tmp_ref)
    inv = tmp_ref[...]
    ritz_ref[...] = nn(nt(stiff_ref[...], inv), inv)


def factor_old(stiff, mass, j_ref, jm_ref, b_ref, tmp_ref):
    n = tmp_ref.shape[0]
    lower_inverse(stiff[:n, :n], tmp_ref)
    first = tmp_ref[...]
    q = nt(stiff[n:, :n], first)
    lower_inverse(stiff[n:, n:] - nt(q, q), tmp_ref)
    second = tmp_ref[...]
    j_ref[:n, :n] = first
    j_ref[:n, n:] = jnp.zeros((n, n), jnp.float32)
    j_ref[n:, :n] = -nn(second, nn(q, first))
    j_ref[n:, n:] = second
    j = j_ref[...]
    jm = nt(mass, j)
    jm_ref[...] = jm
    b_ref[...] = nn(j, jm)


def old_kernel(stiff_ref, mass_ref, j_ref, jm_ref, b_ref, tmp_ref):
    factor_old(stiff_ref[...], mass_ref[...], j_ref, jm_ref, b_ref, tmp_ref)


def carry_kernel(
    y_ref, gxp_ref, mxp_ref, gw_ref, mw_ref, next_ref, j_ref, jm_ref, b_ref, tmp_ref
):
    n = tmp_ref.shape[0]
    ya = y_ref[:, : 2 * n]
    yb = y_ref[:, 2 * n :]
    lane = lax.broadcasted_iota(jnp.int32, ya.shape, 1)
    pa = jnp.concatenate([ya, jnp.where(lane < n, 0.0, ya)], 0)
    pb = jnp.concatenate([yb, yb], 0)

    def turned(old_ref, col_ref):
        col = col_ref[:, : 2 * n]
        ha = nn(pa, old_ref[...]) + nn(pb, col)
        hb = nt(pa, col) + nn(pb, col_ref[:, 2 * n :])
        return nt(ha, pa) + nt(hb, pb)

    mass = turned(mxp_ref, mw_ref)
    next_ref[...] = mass
    factor_old(turned(gxp_ref, gw_ref), mass, j_ref, jm_ref, b_ref, tmp_ref)


def ritz_kernel(
    gw_ref, mw_ref, mxp_ref, j_ref, jm_ref, b_ref, y_ref, ritz_ref, tmp_ref
):
    n = tmp_ref.shape[0]
    j = j_ref[...]
    bxx = b_ref[...]
    qt = nt(gw_ref[:, : 2 * n], j)
    lower_inverse(gw_ref[:, 2 * n :] - nt(qt, qt), tmp_ref)
    lw = tmp_ref[...]
    t = nn(qt, j)
    mwx = mw_ref[:, : 2 * n]
    d = mwx - nn(t, mxp_ref[...])
    e = mw_ref[:, 2 * n :] - nt(t, mwx) - nt(d, t)
    bwx = nn(lw, nt(d, j))
    bww = nt(nn(lw, e), lw)
    va = jm_ref[:n, :]
    vb = jnp.transpose(nn(lw, d[:, :n]))
    ua = ub = None
    for inner_index in range(RR_ITERS):
        wa = nn(va, bxx) + nn(vb, bwx)
        wb = nt(va, bwx) + nn(vb, bww)
        lower_inverse(nt(wa, va) + nt(wb, vb), tmp_ref)
        lc = tmp_ref[...]
        ua, ub = nn(lc, va), nn(lc, vb)
        va, vb = nn(lc, wa), nn(lc, wb)
    ritz_ref[...] = nt(ua, ua) + nt(ub, ub)
    yw = nn(ub, lw)
    y_ref[:, : 2 * n] = nn(ua, j) - nn(yw, t)
    y_ref[:, 2 * n :] = yw


def dense(kernel, shapes, size):
    return pl.pallas_call(
        kernel,
        out_shape=tuple(jax.ShapeDtypeStruct(s, jnp.float32) for s in shapes),
        scratch_shapes=[pltpu.VMEM((size, size), jnp.float32)],
    )


def body(
    x_start,
    p_start,
    k_diag,
    k_link,
    m_diag,
    m_link,
    link_to,
    link_count,
    k_iface,
    m_iface,
    iface_local,
    iface_live,
):
    col_part, row_count = x_start.shape
    modes = col_part * lax.axis_size(COLS)
    dof_count = row_count * lax.axis_size(ROWS)
    node_count, link_slots = link_to.shape
    node_size = k_diag.shape[1]
    node_ids = jnp.arange(node_count, dtype=jnp.int32)
    slot_ids = iface_local.reshape(-1)
    slot_live = iface_live.reshape(-1) > 0
    link_live = jnp.arange(link_slots, dtype=jnp.int32)[None, :] < link_count[:, None]

    def side_by_side(k_part, m_part, live):
        pair = jnp.concatenate([k_part, m_part], 2)
        return jnp.where(live[:, None, None], pair, jnp.zeros_like(pair))

    def flat(blocks):
        return blocks.reshape(-1, node_size, node_size)

    def flipped(blocks):
        return jnp.swapaxes(flat(blocks), 1, 2)

    live_flat = link_live.reshape(-1)
    blocks = jnp.concatenate(
        [
            side_by_side(flat(k_iface), flat(m_iface), slot_live),
            side_by_side(k_diag, m_diag, jnp.ones((node_count,), bool)),
            side_by_side(flipped(k_link), flipped(m_link), live_flat),
            side_by_side(flat(k_link), flat(m_link), live_flat),
        ],
        0,
    )
    link_from = jnp.repeat(node_ids, link_slots)
    link_flat = link_to.reshape(-1)
    src_ids = jnp.concatenate([node_ids, link_flat, link_from])
    dst_ids = jnp.concatenate([slot_ids, node_ids, link_from, link_flat])
    src_onehot = (src_ids[:, None] == node_ids[None, :]).astype(jnp.float32)
    dst_onehot = (dst_ids[:, None] == node_ids[None, :]).astype(jnp.float32)
    tables = (blocks, src_onehot, dst_onehot, node_count)

    precond = 1.0 / jnp.diagonal(k_diag.astype(jnp.float32), axis1=1, axis2=2).reshape(-1)
    col_start = lax.axis_index(COLS) * col_part

    start = jnp.concatenate([x_start, p_start], 0)
    received = exchange(start, slot_ids, node_count)
    all_x, all_p = gather_cols(x_start, p_start)
    own_k, own_m = apply_pair(start, received, tables)
    products = (own_k[:col_part], own_m[:col_part], own_k[col_part:], own_m[col_part:])
    gram = reduce_gram(
        jnp.concatenate([all_x, all_p], 0), jnp.concatenate(products, 0), dof_count
    )
    all_kx, all_mx, all_kp, all_mp = gather_cols(*products)

    def block(gram, position):
        piece = gram[:, position * col_part : (position + 1) * col_part]
        return piece.reshape(modes, piece.shape[2])

    square = (modes, modes)
    pair = (2 * modes, 2 * modes)
    old_stiff = jnp.concatenate([block(gram, 0), block(gram, 2)], 0)
    old_mass = jnp.concatenate([block(gram, 1), block(gram, 3)], 0)
    (ritz_turned,) = dense(first_ritz_kernel, (square,), modes)(
        old_stiff[:modes, :modes], old_mass[:modes, :modes]
    )
    factors = dense(old_kernel, (pair,) * 3, modes)(old_stiff, old_mass)
    for step_index in range(STEPS):
        all_w = (all_kx - edot(ritz_turned, all_mx)) * precond[None, :]
        own_w = lax.dynamic_slice_in_dim(all_w, col_start, col_part, 0)
        received = exchange(own_w, slot_ids, node_count)
        received, old_mass, factors = lax.optimization_barrier((received, old_mass, factors))
        own_kw, own_mw = apply_pair(own_w, received, tables)
        space = jnp.concatenate([all_x, all_p, all_w], 0)
        gram = reduce_gram(space, jnp.concatenate([own_kw, own_mw], 0), dof_count)
        stiff_w, mass_w = block(gram, 0), block(gram, 1)
        coeffs, ritz_turned = dense(ritz_kernel, ((modes, 3 * modes), square), modes)(
            stiff_w, mass_w, old_mass, *factors
        )
        if step_index + 1 == STEPS:
            mine = lax.dynamic_slice_in_dim(coeffs, col_start, col_part, 0)
            p_out = edot(mine[:, modes:], space[modes:])
            x_out = p_out + edot(mine[:, :modes], space[:modes])
            return (x_out, p_out, ritz_turned)
        all_kw, all_mw = gather_cols(own_kw, own_mw)
        wide_x = jnp.concatenate([all_kx, all_mx, all_x], 1)
        wide_rest = jnp.concatenate(
            [
                jnp.concatenate([all_kp, all_mp, all_p], 1),
                jnp.concatenate([all_kw, all_mw, all_w], 1),
            ],
            0,
        )
        new_p = edot(coeffs[:, modes:], wide_rest)
        new_x = new_p + edot(coeffs[:, :modes], wide_x)
        all_kx, all_mx, all_x = [new_x[:, i * row_count : (i + 1) * row_count] for i in range(3)]
        all_p = new_p[:, 2 * row_count :]
        old_mass, *factors = dense(carry_kernel, (pair,) * 4, modes)(
            coeffs, old_stiff, old_mass, stiff_w, mass_w
        )


def solution(mesh):
    rows, cols = mesh.devices.shape
    fine = Mesh(
        mesh.devices.reshape(rows // Y_SIZE, Y_SIZE, cols // CORES, CORES), ROWS + COLS
    )
    placed = (P(COLS, ROWS),) * 2 + (P(ROWS),) * 10
    return jax.shard_map(
        body,
        mesh=fine,
        in_specs=placed,
        out_specs=(P(COLS, ROWS), P(COLS, ROWS), P()),
        check_vma=False,
    )
```

```python
import functools

import jax
import jax.numpy as jnp
from jax import lax
from jax.experimental import pallas as pl
from jax.experimental.pallas import tpu as pltpu
from jax.sharding import Mesh, PartitionSpec as P

ROWS = ("z", "y")
COLS = ("x", "core")
Y_SIZE = 4
CORES = 2
STEPS = 2
RR_ITERS = 3
GROUP = 8


exact_dots = lax.Precision.HIGHEST


def edot(a, b):
    return jnp.dot(a, b, precision=exact_dots)


def swap(array, axis):
    return lax.all_to_all(array, axis, split_axis=0, concat_axis=0, tiled=True)


def spread(array, axis):
    count = lax.axis_size(axis)
    return swap(jnp.broadcast_to(array[None], (count,) + array.shape), axis)


def gather_cols(*blocks):
    count = blocks[0].shape[0]
    moved = lax.all_gather(jnp.concatenate(blocks, 0), COLS, axis=0)
    return [
        moved[:, i * count : (i + 1) * count].reshape(-1, blocks[0].shape[1])
        for i in range(len(blocks))
    ]


def reduce_gram(part):
    piece = jnp.sum(swap(part.reshape(lax.axis_size("y"), -1), "y"), 0)
    piece = jnp.sum(spread(piece, "z"), 0)
    whole = spread(piece, ("y",) + COLS)
    whole = whole.reshape(lax.axis_size("y"), lax.axis_size(COLS), -1, part.shape[1])
    return jnp.swapaxes(whole, 0, 1).reshape((-1,) + part.shape)


def nn(a, b):
    return lax.dot_general(
        a, b, (((1,), (0,)), ((), ())), precision=exact_dots, preferred_element_type=jnp.float32
    )


def nt(a, b):
    return lax.dot_general(
        a, b, (((1,), (1,)), ((), ())), precision=exact_dots, preferred_element_type=jnp.float32
    )


def node_rows(vec_ref, node_ref):
    half = vec_ref.shape[0] // 2
    size = vec_ref.shape[1] // node_ref.shape[0]
    for s in range(node_ref.shape[0]):
        both = [vec_ref[h * half : (h + 1) * half, s * size : (s + 1) * size] for h in range(2)]
        node_ref[s] = jnp.concatenate(both, 1)


def pick_kernel(slot_ref, vec_ref, out_ref, node_ref):
    node_rows(vec_ref, node_ref)
    rows = node_ref.shape[1]

    def group(g, carry):
        first = pl.multiple_of(g * (rows * GROUP), 8)
        pieces = [node_ref[slot_ref[g * GROUP + i]] for i in range(GROUP)]
        out_ref[pl.ds(first, rows * GROUP), :] = jnp.concatenate(pieces, 0)
        return carry

    lax.fori_loop(0, out_ref.shape[0] // (rows * GROUP), group, 0, unroll=2)


def apply_kernel(
    dof_count,
    dst_ref,
    src_ref,
    recv_ref,
    vec_ref,
    blocks_ref,
    space_ref,
    own_ref,
    part_ref,
    node_ref,
    acc_ref,
):
    node_rows(vec_ref, node_ref)
    nodes, rows, lanes = node_ref.shape
    padded = acc_ref.shape[1] // 2
    size = lanes // 2
    acc_ref[...] = jnp.zeros(acc_ref.shape, jnp.float32)
    fill = jnp.zeros((padded - rows, lanes), jnp.float32)

    def add(piece, slot):
        full = jnp.concatenate([piece, fill], 0)
        pair = jnp.concatenate([full, pltpu.roll(full, size, 1)], 0)[:, :size]
        high = pair.astype(jnp.bfloat16)
        rest = pair - high.astype(jnp.float32)
        middle = rest.astype(jnp.bfloat16)
        low = (rest - middle.astype(jnp.float32)).astype(jnp.bfloat16)
        terms = jnp.concatenate([high, middle, low], 0)
        out = jnp.dot(terms, blocks_ref[slot], preferred_element_type=jnp.float32)
        two = 2 * padded
        node = dst_ref[slot]
        acc_ref[node] = acc_ref[node] + (out[:two] + out[two : 2 * two] + out[2 * two :])

    def faces(g, carry):
        first = pl.multiple_of(g * (rows * GROUP), 8)
        chunk = recv_ref[pl.ds(first, rows * GROUP), :]
        for i in range(GROUP):
            add(chunk[rows * i : rows * (i + 1)], g * GROUP + i)
        return carry

    count = recv_ref.shape[0] // rows
    lax.fori_loop(0, count // GROUP, faces, 0)

    def local(g, carry):
        for i in range(GROUP):
            k = g * GROUP + i
            add(node_ref[src_ref[k]], count + k)
        return carry

    lax.fori_loop(0, src_ref.shape[0] // GROUP, local, 0)
    for which in range(2):
        for h in range(2):
            row = which * 2 * rows + h * rows
            for s in range(nodes):
                own_ref[row : row + rows, s * size : (s + 1) * size] = acc_ref[
                    s, h * padded : h * padded + rows, which * size : (which + 1) * size
                ]
    part_ref[...] = nt(own_ref[...], space_ref[...]) / dof_count


def at(*spaces):
    return [pl.BlockSpec(memory_space=space) for space in spaces]


def exchange(vectors, slot_ids, node_count):
    rows = vectors.shape[0] // 2
    lanes = 2 * vectors.shape[1] // node_count
    picked = pl.pallas_call(
        pick_kernel,
        out_shape=jax.ShapeDtypeStruct((slot_ids.shape[0] * rows, lanes), jnp.float32),
        in_specs=at(pltpu.SMEM, pltpu.VMEM),
        out_specs=at(pltpu.VMEM)[0],
        scratch_shapes=[pltpu.VMEM((node_count, rows, lanes), jnp.float32)],
    )(slot_ids, vectors)
    owners = lax.axis_size(ROWS)
    return swap(picked.reshape(owners, -1), ROWS).reshape(picked.shape)


def apply_pair(vectors, received, tables, space, dof_count):
    blocks, src_ids, dst_ids, node_count = tables
    col_count, row_count = vectors.shape
    rows = col_count // 2
    lanes = 2 * row_count // node_count
    padded = -(-rows // 8) * 8
    shapes = ((2 * col_count, row_count), (2 * col_count, space.shape[0]))
    return pl.pallas_call(
        functools.partial(apply_kernel, dof_count),
        out_shape=tuple(jax.ShapeDtypeStruct(s, jnp.float32) for s in shapes),
        in_specs=at(pltpu.SMEM, pltpu.SMEM, *(pltpu.VMEM,) * 4),
        out_specs=at(pltpu.VMEM, pltpu.VMEM),
        scratch_shapes=[
            pltpu.VMEM((node_count, rows, lanes), jnp.float32),
            pltpu.VMEM((node_count, 2 * padded, lanes), jnp.float32),
        ],
        compiler_params=pltpu.CompilerParams(vmem_limit_bytes=40 * 2**20),
    )(dst_ids, src_ids, received, vectors, blocks, space)


LANES = 128
PANEL = 8

def lower_inverse(matrix, out_ref):
    size = matrix.shape[0]
    tiles = size // PANEL
    wide = jnp.concatenate([matrix, jnp.zeros((size, LANES - size), jnp.float32)], 1)
    row = lax.broadcasted_iota(jnp.int32, (size, LANES), 0)
    lane = lax.broadcasted_iota(jnp.int32, (size, LANES), 1)
    ident = jnp.where(row == lane, 1.0, 0.0).astype(jnp.float32)
    left = [wide[PANEL * t : PANEL * t + PANEL] for t in range(tiles)]
    right = [ident[PANEL * t : PANEL * t + PANEL] for t in range(tiles)]
    full = (PANEL, LANES)

    def lane_splat(tile, k):
        return jnp.broadcast_to(tile[:, k : k + 1], full)

    def row_splat(tile, i):
        return jnp.broadcast_to(tile[i : i + 1, :], full)

    for p in range(tiles):
        base = PANEL * p
        cols = [lane_splat(left[p], base + k) for k in range(PANEL)]
        s = {(i, k): row_splat(cols[k], i) for k in range(PANEL) for i in range(k, PANEL)}
        low = {}
        inv = {}
        for k in range(PANEL):
            d = s[k, k]
            r = lax.rsqrt(d)
            r = r * (1.5 - 0.5 * d * r * r)
            inv[k, k] = r
            for i in range(k + 1, PANEL):
                low[i, k] = s[i, k] * r
            for m in range(k + 1, PANEL):
                for i in range(m, PANEL):
                    s[i, m] = s[i, m] - low[i, k] * low[m, k]
        for i in range(1, PANEL):
            for j in range(i):
                acc = low[i, j] * inv[j, j]
                for k in range(j + 1, i):
                    acc = acc + low[i, k] * inv[k, j]
                inv[i, j] = -inv[i, i] * acc
        rows_l = [row_splat(left[p], i) for i in range(PANEL)]
        rows_r = [row_splat(right[p], i) for i in range(PANEL)]
        new_l, new_r = [], []
        for i in range(PANEL):
            al = inv[i, 0] * rows_l[0]
            ar = inv[i, 0] * rows_r[0]
            for k in range(1, i + 1):
                al = al + inv[i, k] * rows_l[k]
                ar = ar + inv[i, k] * rows_r[k]
            new_l.append(al)
            new_r.append(ar)
            out_ref[base + i : base + i + 1, :] = ar[0:1, :size]
        for t in range(p + 1, tiles):
            ct = [lane_splat(left[t], base + k) for k in range(PANEL)]
            for k in range(PANEL):
                f = inv[k, 0] * ct[0]
                for j in range(1, k + 1):
                    f = f + inv[k, j] * ct[j]
                left[t] = left[t] - f * new_l[k]
                right[t] = right[t] - f * new_r[k]


def first_ritz_kernel(stiff_ref, mass_ref, ritz_ref, tmp_ref):
    lower_inverse(mass_ref[...], tmp_ref)
    inv = tmp_ref[...]
    ritz_ref[...] = nn(nt(stiff_ref[...], inv), inv)


def factor_old(stiff, mass, j_ref, jm_ref, b_ref, tmp_ref):
    n = tmp_ref.shape[0]
    lower_inverse(stiff[:n, :n], tmp_ref)
    first = tmp_ref[...]
    q = nt(stiff[n:, :n], first)
    lower_inverse(stiff[n:, n:] - nt(q, q), tmp_ref)
    second = tmp_ref[...]
    j_ref[:n, :n] = first
    j_ref[:n, n:] = jnp.zeros((n, n), jnp.float32)
    j_ref[n:, :n] = -nn(second, nn(q, first))
    j_ref[n:, n:] = second
    j = j_ref[...]
    jm = nt(mass, j)
    jm_ref[...] = jm
    b_ref[...] = nn(j, jm)


def old_kernel(stiff_ref, mass_ref, j_ref, jm_ref, b_ref, tmp_ref):
    factor_old(stiff_ref[...], mass_ref[...], j_ref, jm_ref, b_ref, tmp_ref)


def carry_kernel(
    y_ref, gxp_ref, mxp_ref, gw_ref, mw_ref, next_ref, j_ref, jm_ref, b_ref, tmp_ref
):
    n = tmp_ref.shape[0]
    ya = y_ref[:, : 2 * n]
    yb = y_ref[:, 2 * n :]
    lane = lax.broadcasted_iota(jnp.int32, ya.shape, 1)
    pa = jnp.concatenate([ya, jnp.where(lane < n, 0.0, ya)], 0)
    pb = jnp.concatenate([yb, yb], 0)

    def turned(old_ref, col_ref):
        col = col_ref[:, : 2 * n]
        ha = nn(pa, old_ref[...]) + nn(pb, col)
        hb = nt(pa, col) + nn(pb, col_ref[:, 2 * n :])
        return nt(ha, pa) + nt(hb, pb)

    mass = turned(mxp_ref, mw_ref)
    next_ref[...] = mass
    factor_old(turned(gxp_ref, gw_ref), mass, j_ref, jm_ref, b_ref, tmp_ref)


def ritz_kernel(
    gw_ref, mw_ref, mxp_ref, j_ref, jm_ref, b_ref, y_ref, ritz_ref, tmp_ref
):
    n = tmp_ref.shape[0]
    j = j_ref[...]
    bxx = b_ref[...]
    qt = nt(gw_ref[:, : 2 * n], j)
    lower_inverse(gw_ref[:, 2 * n :] - nt(qt, qt), tmp_ref)
    lw = tmp_ref[...]
    t = nn(qt, j)
    mwx = mw_ref[:, : 2 * n]
    d = mwx - nn(t, mxp_ref[...])
    e = mw_ref[:, 2 * n :] - nt(t, mwx) - nt(d, t)
    bwx = nn(lw, nt(d, j))
    bww = nt(nn(lw, e), lw)
    va = jm_ref[:n, :]
    vb = jnp.transpose(nn(lw, d[:, :n]))
    ua = ub = None
    for inner_index in range(RR_ITERS):
        wa = nn(va, bxx) + nn(vb, bwx)
        wb = nt(va, bwx) + nn(vb, bww)
        lower_inverse(nt(wa, va) + nt(wb, vb), tmp_ref)
        lc = tmp_ref[...]
        ua, ub = nn(lc, va), nn(lc, vb)
        va, vb = nn(lc, wa), nn(lc, wb)
    ritz_ref[...] = nt(ua, ua) + nt(ub, ub)
    yw = nn(ub, lw)
    y_ref[:, : 2 * n] = nn(ua, j) - nn(yw, t)
    y_ref[:, 2 * n :] = yw


def dense(kernel, shapes, size):
    return pl.pallas_call(
        kernel,
        out_shape=tuple(jax.ShapeDtypeStruct(s, jnp.float32) for s in shapes),
        scratch_shapes=[pltpu.VMEM((size, size), jnp.float32)],
    )


def body(
    x_start,
    p_start,
    k_diag,
    k_link,
    m_diag,
    m_link,
    link_to,
    link_count,
    k_iface,
    m_iface,
    iface_local,
    iface_live,
):
    col_part, row_count = x_start.shape
    modes = col_part * lax.axis_size(COLS)
    dof_count = row_count * lax.axis_size(ROWS)
    node_count, link_slots = link_to.shape
    node_size = k_diag.shape[1]
    node_ids = jnp.arange(node_count, dtype=jnp.int32)
    slot_ids = iface_local.reshape(-1)
    slot_live = iface_live.reshape(-1) > 0
    link_live = jnp.arange(link_slots, dtype=jnp.int32)[None, :] < link_count[:, None]

    def side_by_side(k_part, m_part, live):
        pair = jnp.concatenate([k_part, m_part], 2)
        return jnp.where(live[:, None, None], pair, jnp.zeros_like(pair))

    def flat(blocks):
        return blocks.reshape(-1, node_size, node_size)

    def flipped(blocks):
        return jnp.swapaxes(flat(blocks), 1, 2)

    live_flat = link_live.reshape(-1)
    blocks = jnp.concatenate(
        [
            side_by_side(flat(k_iface), flat(m_iface), slot_live),
            side_by_side(k_diag, m_diag, jnp.ones((node_count,), bool)),
            side_by_side(flipped(k_link), flipped(m_link), live_flat),
            side_by_side(flat(k_link), flat(m_link), live_flat),
        ],
        0,
    )
    link_from = jnp.repeat(node_ids, link_slots)
    link_flat = link_to.reshape(-1)
    src_ids = jnp.concatenate([node_ids, link_flat, link_from])
    dst_ids = jnp.concatenate([slot_ids, node_ids, link_from, link_flat])
    tables = (blocks, src_ids, dst_ids, node_count)

    precond = 1.0 / jnp.diagonal(k_diag.astype(jnp.float32), axis1=1, axis2=2).reshape(-1)
    col_start = lax.axis_index(COLS) * col_part

    start = jnp.concatenate([x_start, p_start], 0)
    received = exchange(start, slot_ids, node_count)
    all_x, all_p = gather_cols(x_start, p_start)
    own, part = apply_pair(
        start, received, tables, jnp.concatenate([all_x, all_p], 0), dof_count
    )
    gram = reduce_gram(part)
    all_kx, all_kp, all_mx, all_mp = gather_cols(
        *[own[i * col_part : (i + 1) * col_part] for i in range(4)]
    )

    def block(gram, position):
        piece = gram[:, position * col_part : (position + 1) * col_part]
        return piece.reshape(modes, piece.shape[2])

    square = (modes, modes)
    pair = (2 * modes, 2 * modes)
    old_stiff = jnp.concatenate([block(gram, 0), block(gram, 1)], 0)
    old_mass = jnp.concatenate([block(gram, 2), block(gram, 3)], 0)
    (ritz_turned,) = dense(first_ritz_kernel, (square,), modes)(
        old_stiff[:modes, :modes], old_mass[:modes, :modes]
    )
    factors = dense(old_kernel, (pair,) * 3, modes)(old_stiff, old_mass)
    for step_index in range(STEPS):
        all_w = (all_kx - edot(ritz_turned, all_mx)) * precond[None, :]
        own_w = lax.dynamic_slice_in_dim(all_w, col_start, col_part, 0)
        received = exchange(own_w, slot_ids, node_count)
        received, old_mass, factors = lax.optimization_barrier((received, old_mass, factors))
        space = jnp.concatenate([all_x, all_p, all_w], 0)
        own, part = apply_pair(own_w, received, tables, space, dof_count)
        gram = reduce_gram(part)
        stiff_w, mass_w = block(gram, 0), block(gram, 1)
        coeffs, ritz_turned = dense(ritz_kernel, ((modes, 3 * modes), square), modes)(
            stiff_w, mass_w, old_mass, *factors
        )
        if step_index + 1 == STEPS:
            mine = lax.dynamic_slice_in_dim(coeffs, col_start, col_part, 0)
            p_out = edot(mine[:, modes:], space[modes:])
            x_out = p_out + edot(mine[:, :modes], space[:modes])
            return (x_out, p_out, ritz_turned)
        all_kw, all_mw = gather_cols(own[:col_part], own[col_part:])
        wide_x = jnp.concatenate([all_kx, all_mx, all_x], 1)
        wide_rest = jnp.concatenate(
            [
                jnp.concatenate([all_kp, all_mp, all_p], 1),
                jnp.concatenate([all_kw, all_mw, all_w], 1),
            ],
            0,
        )
        new_p = edot(coeffs[:, modes:], wide_rest)
        new_x = new_p + edot(coeffs[:, :modes], wide_x)
        all_kx, all_mx, all_x = [new_x[:, i * row_count : (i + 1) * row_count] for i in range(3)]
        all_p = new_p[:, 2 * row_count :]
        old_mass, *factors = dense(carry_kernel, (pair,) * 4, modes)(
            coeffs, old_stiff, old_mass, stiff_w, mass_w
        )


def solution(mesh):
    rows, cols = mesh.devices.shape
    fine = Mesh(
        mesh.devices.reshape(rows // Y_SIZE, Y_SIZE, cols // CORES, CORES), ROWS + COLS
    )
    placed = (P(COLS, ROWS),) * 2 + (P(ROWS),) * 10
    return jax.shard_map(
        body,
        mesh=fine,
        in_specs=placed,
        out_specs=(P(COLS, ROWS), P(COLS, ROWS), P()),
        check_vma=False,
    )
```

```python
import functools

import jax
import jax.numpy as jnp
from jax import lax
from jax.experimental import pallas as pl
from jax.experimental.pallas import tpu as pltpu
from jax.sharding import Mesh, PartitionSpec as P

ROWS = ("z", "y")
COLS = ("x", "core")
Y_SIZE = 4
CORES = 2
STEPS = 2
RR_ITERS = 3
GROUP = 8


exact_dots = lax.Precision.HIGHEST


def edot(a, b):
    return jnp.dot(a, b, precision=exact_dots)


def swap(array, axis):
    return lax.all_to_all(array, axis, split_axis=0, concat_axis=0, tiled=True)


def spread(array, axis):
    count = lax.axis_size(axis)
    return swap(jnp.broadcast_to(array[None], (count,) + array.shape), axis)


def gather_cols(*blocks):
    count = blocks[0].shape[0]
    moved = lax.all_gather(jnp.concatenate(blocks, 0), COLS, axis=0)
    return [
        moved[:, i * count : (i + 1) * count].reshape(-1, blocks[0].shape[1])
        for i in range(len(blocks))
    ]


def reduce_gram(part, beside):
    piece = jnp.sum(swap(part.reshape(lax.axis_size("y"), -1), "y"), 0)
    piece = jnp.sum(spread(piece, "z"), 0)
    piece, beside = lax.optimization_barrier((piece, beside))
    whole = spread(piece, ("y",) + COLS)
    whole = whole.reshape(lax.axis_size("y"), lax.axis_size(COLS), -1, part.shape[1])
    return jnp.swapaxes(whole, 0, 1).reshape((-1,) + part.shape), beside


def nn(a, b):
    return lax.dot_general(
        a, b, (((1,), (0,)), ((), ())), precision=exact_dots, preferred_element_type=jnp.float32
    )


def nt(a, b):
    return lax.dot_general(
        a, b, (((1,), (1,)), ((), ())), precision=exact_dots, preferred_element_type=jnp.float32
    )


def node_rows(vec_ref, node_ref):
    half = vec_ref.shape[0] // 2
    size = vec_ref.shape[1] // node_ref.shape[0]
    for s in range(node_ref.shape[0]):
        both = [vec_ref[h * half : (h + 1) * half, s * size : (s + 1) * size] for h in range(2)]
        node_ref[s] = jnp.concatenate(both, 1)


def pick_kernel(slot_ref, vec_ref, out_ref, node_ref):
    node_rows(vec_ref, node_ref)
    rows = node_ref.shape[1]

    def group(g, carry):
        first = pl.multiple_of(g * (rows * GROUP), 8)
        pieces = [node_ref[slot_ref[g * GROUP + i]] for i in range(GROUP)]
        out_ref[pl.ds(first, rows * GROUP), :] = jnp.concatenate(pieces, 0)
        return carry

    lax.fori_loop(0, out_ref.shape[0] // (rows * GROUP), group, 0, unroll=2)


def add_product(acc_ref, node, piece, block):
    rows, lanes = piece.shape
    padded = acc_ref.shape[1] // 2
    fill = jnp.zeros((padded - rows, lanes), jnp.float32)
    full = jnp.concatenate([piece, fill], 0)
    half = lanes // 2
    pair = jnp.concatenate([full, pltpu.roll(full, half, 1)], 0)[:, :half]
    high = pair.astype(jnp.bfloat16)
    rest = pair - high.astype(jnp.float32)
    middle = rest.astype(jnp.bfloat16)
    low = (rest - middle.astype(jnp.float32)).astype(jnp.bfloat16)
    terms = jnp.concatenate([high, middle, low], 0)
    out = jnp.dot(terms, block, preferred_element_type=jnp.float32)
    two = 2 * padded
    acc_ref[node] = acc_ref[node] + (out[:two] + out[two : 2 * two] + out[2 * two :])


def local_kernel(dst_ref, src_ref, vec_ref, blocks_ref, acc_ref, node_ref):
    node_rows(vec_ref, node_ref)
    acc_ref[...] = jnp.zeros(acc_ref.shape, jnp.float32)

    def group(g, carry):
        for i in range(GROUP):
            k = g * GROUP + i
            add_product(acc_ref, dst_ref[k], node_ref[src_ref[k]], blocks_ref[k])
        return carry

    lax.fori_loop(0, src_ref.shape[0] // GROUP, group, 0)


def face_kernel(
    dof_count, dst_ref, recv_ref, start_ref, blocks_ref, space_ref, own_ref, part_ref, acc_ref
):
    slots = dst_ref.shape[0]
    rows = recv_ref.shape[0] // slots
    nodes, two, lanes = acc_ref.shape
    padded = two // 2
    size = lanes // 2
    acc_ref[...] = start_ref[...]

    def group(g, carry):
        first = pl.multiple_of(g * (rows * GROUP), 8)
        chunk = recv_ref[pl.ds(first, rows * GROUP), :]
        for i in range(GROUP):
            k = g * GROUP + i
            add_product(acc_ref, dst_ref[k], chunk[rows * i : rows * (i + 1)], blocks_ref[k])
        return carry

    lax.fori_loop(0, slots // GROUP, group, 0)
    for which in range(2):
        for h in range(2):
            row = which * 2 * rows + h * rows
            for s in range(nodes):
                own_ref[row : row + rows, s * size : (s + 1) * size] = acc_ref[
                    s, h * padded : h * padded + rows, which * size : (which + 1) * size
                ]
    part_ref[...] = nt(own_ref[...], space_ref[...]) / dof_count


def at(*spaces):
    return [pl.BlockSpec(memory_space=space) for space in spaces]


def exchange(vectors, slot_ids, node_count):
    rows = vectors.shape[0] // 2
    lanes = 2 * vectors.shape[1] // node_count
    picked = pl.pallas_call(
        pick_kernel,
        out_shape=jax.ShapeDtypeStruct((slot_ids.shape[0] * rows, lanes), jnp.float32),
        in_specs=at(pltpu.SMEM, pltpu.VMEM),
        out_specs=at(pltpu.VMEM)[0],
        scratch_shapes=[pltpu.VMEM((node_count, rows, lanes), jnp.float32)],
    )(slot_ids, vectors)
    owners = lax.axis_size(ROWS)
    return swap(picked.reshape(owners, -1), ROWS).reshape(picked.shape)


def apply_local(vectors, tables):
    blocks, src_ids, dst_ids, node_count = tables
    col_count, row_count = vectors.shape
    rows = col_count // 2
    lanes = 2 * row_count // node_count
    padded = -(-rows // 8) * 8
    return pl.pallas_call(
        local_kernel,
        out_shape=jax.ShapeDtypeStruct((node_count, 2 * padded, lanes), jnp.float32),
        in_specs=at(pltpu.SMEM, pltpu.SMEM, pltpu.VMEM, pltpu.VMEM),
        out_specs=at(pltpu.VMEM)[0],
        scratch_shapes=[pltpu.VMEM((node_count, rows, lanes), jnp.float32)],
        compiler_params=pltpu.CompilerParams(vmem_limit_bytes=16 * 2**20),
    )(dst_ids, src_ids, vectors, blocks)


def apply_faces(local, received, blocks, slot_ids, space, dof_count):
    col_count = 2 * received.shape[0] // slot_ids.shape[0]
    shapes = ((2 * col_count, space.shape[1]), (2 * col_count, space.shape[0]))
    return pl.pallas_call(
        functools.partial(face_kernel, dof_count),
        out_shape=tuple(jax.ShapeDtypeStruct(s, jnp.float32) for s in shapes),
        in_specs=at(pltpu.SMEM, *(pltpu.VMEM,) * 4),
        out_specs=at(pltpu.VMEM, pltpu.VMEM),
        scratch_shapes=[pltpu.VMEM(local.shape, jnp.float32)],
        compiler_params=pltpu.CompilerParams(vmem_limit_bytes=16 * 2**20),
    )(slot_ids, received, local, blocks, space)


LANES = 128
PANEL = 8

def lower_inverse(matrix, out_ref):
    size = matrix.shape[0]
    tiles = size // PANEL
    wide = jnp.concatenate([matrix, jnp.zeros((size, LANES - size), jnp.float32)], 1)
    row = lax.broadcasted_iota(jnp.int32, (size, LANES), 0)
    lane = lax.broadcasted_iota(jnp.int32, (size, LANES), 1)
    ident = jnp.where(row == lane, 1.0, 0.0).astype(jnp.float32)
    left = [wide[PANEL * t : PANEL * t + PANEL] for t in range(tiles)]
    right = [ident[PANEL * t : PANEL * t + PANEL] for t in range(tiles)]
    full = (PANEL, LANES)

    def lane_splat(tile, k):
        return jnp.broadcast_to(tile[:, k : k + 1], full)

    def row_splat(tile, i):
        return jnp.broadcast_to(tile[i : i + 1, :], full)

    for p in range(tiles):
        base = PANEL * p
        cols = [lane_splat(left[p], base + k) for k in range(PANEL)]
        s = {(i, k): row_splat(cols[k], i) for k in range(PANEL) for i in range(k, PANEL)}
        rows_l = [row_splat(left[p], i) for i in range(PANEL)]
        rows_r = [row_splat(right[p], i) for i in range(PANEL)]
        later = range(p + 1, min(p + 2, tiles))
        below = {t: [lane_splat(left[t], base + k) for k in range(PANEL)] for t in later}
        lows, roots, outs = [], [], []
        for k in range(PANEL):
            r = lax.rsqrt(s[k, k])
            low = {i: s[i, k] * r for i in range(k + 1, PANEL)}
            for m in range(k + 1, PANEL):
                for i in range(m, PANEL):
                    s[i, m] = s[i, m] - low[i] * low[m]
            new_l = rows_l[k] * r
            new_r = rows_r[k] * r
            out_ref[base + k : base + k + 1, :] = new_r[0:1, :size]
            for i in range(k + 1, PANEL):
                rows_l[i] = rows_l[i] - low[i] * new_l
                rows_r[i] = rows_r[i] - low[i] * new_r
            for t in later:
                factor = below[t][k] * r
                for i in range(k + 1, PANEL):
                    below[t][i] = below[t][i] - low[i] * factor
                left[t] = left[t] - factor * new_l
                right[t] = right[t] - factor * new_r
            lows.append(low)
            roots.append(r)
            outs.append((new_l, new_r))
        for t in range(p + 2, tiles):
            factors = [lane_splat(left[t], base + k) for k in range(PANEL)]
            for k in range(PANEL):
                factors[k] = factors[k] * roots[k]
                for i in range(k + 1, PANEL):
                    factors[i] = factors[i] - lows[k][i] * factors[k]
                left[t] = left[t] - factors[k] * outs[k][0]
                right[t] = right[t] - factors[k] * outs[k][1]


def first_ritz_kernel(stiff_ref, mass_ref, ritz_ref, tmp_ref):
    lower_inverse(mass_ref[...], tmp_ref)
    inv = tmp_ref[...]
    ritz_ref[...] = nn(nt(stiff_ref[...], inv), inv)


def factor_old(stiff, mass, j_ref, jm_ref, b_ref, tmp_ref):
    n = tmp_ref.shape[0]
    lower_inverse(stiff[:n, :n], tmp_ref)
    first = tmp_ref[...]
    q = nt(stiff[n:, :n], first)
    lower_inverse(stiff[n:, n:] - nt(q, q), tmp_ref)
    second = tmp_ref[...]
    j_ref[:n, :n] = first
    j_ref[:n, n:] = jnp.zeros((n, n), jnp.float32)
    j_ref[n:, :n] = -nn(second, nn(q, first))
    j_ref[n:, n:] = second
    j = j_ref[...]
    jm = nt(mass, j)
    jm_ref[...] = jm
    b_ref[...] = nn(j, jm)


def old_kernel(stiff_ref, mass_ref, j_ref, jm_ref, b_ref, tmp_ref):
    factor_old(stiff_ref[...], mass_ref[...], j_ref, jm_ref, b_ref, tmp_ref)


def carry_kernel(
    y_ref, gxp_ref, mxp_ref, gw_ref, mw_ref, next_ref, j_ref, jm_ref, b_ref, tmp_ref
):
    n = tmp_ref.shape[0]
    ya = y_ref[:, : 2 * n]
    yb = y_ref[:, 2 * n :]
    lane = lax.broadcasted_iota(jnp.int32, ya.shape, 1)
    pa = jnp.concatenate([ya, jnp.where(lane < n, 0.0, ya)], 0)
    pb = jnp.concatenate([yb, yb], 0)

    def turned(old_ref, col_ref):
        col = col_ref[:, : 2 * n]
        ha = nn(pa, old_ref[...]) + nn(pb, col)
        hb = nt(pa, col) + nn(pb, col_ref[:, 2 * n :])
        return nt(ha, pa) + nt(hb, pb)

    mass = turned(mxp_ref, mw_ref)
    next_ref[...] = mass
    factor_old(turned(gxp_ref, gw_ref), mass, j_ref, jm_ref, b_ref, tmp_ref)


def ritz_kernel(
    gw_ref, mw_ref, mxp_ref, j_ref, jm_ref, b_ref, y_ref, ritz_ref, tmp_ref
):
    n = tmp_ref.shape[0]
    j = j_ref[...]
    bxx = b_ref[...]
    qt = nt(gw_ref[:, : 2 * n], j)
    lower_inverse(gw_ref[:, 2 * n :] - nt(qt, qt), tmp_ref)
    lw = tmp_ref[...]
    t = nn(qt, j)
    mwx = mw_ref[:, : 2 * n]
    d = mwx - nn(t, mxp_ref[...])
    e = mw_ref[:, 2 * n :] - nt(t, mwx) - nt(d, t)
    bwx = nn(lw, nt(d, j))
    bww = nt(nn(lw, e), lw)
    va = jm_ref[:n, :]
    vb = jnp.transpose(nn(lw, d[:, :n]))
    ua = ub = None
    for inner_index in range(RR_ITERS):
        wa = nn(va, bxx) + nn(vb, bwx)
        wb = nt(va, bwx) + nn(vb, bww)
        lower_inverse(nt(wa, va) + nt(wb, vb), tmp_ref)
        lc = tmp_ref[...]
        ua, ub = nn(lc, va), nn(lc, vb)
        va, vb = nn(lc, wa), nn(lc, wb)
    ritz_ref[...] = nt(ua, ua) + nt(ub, ub)
    yw = nn(ub, lw)
    y_ref[:, : 2 * n] = nn(ua, j) - nn(yw, t)
    y_ref[:, 2 * n :] = yw


def dense(kernel, shapes, size):
    return pl.pallas_call(
        kernel,
        out_shape=tuple(jax.ShapeDtypeStruct(s, jnp.float32) for s in shapes),
        scratch_shapes=[pltpu.VMEM((size, size), jnp.float32)],
    )


def body(
    x_start,
    p_start,
    k_diag,
    k_link,
    m_diag,
    m_link,
    link_to,
    link_count,
    k_iface,
    m_iface,
    iface_local,
    iface_live,
):
    col_part, row_count = x_start.shape
    modes = col_part * lax.axis_size(COLS)
    dof_count = row_count * lax.axis_size(ROWS)
    node_count, link_slots = link_to.shape
    node_size = k_diag.shape[1]
    node_ids = jnp.arange(node_count, dtype=jnp.int32)
    slot_ids = iface_local.reshape(-1)
    slot_live = iface_live.reshape(-1) > 0
    link_live = jnp.arange(link_slots, dtype=jnp.int32)[None, :] < link_count[:, None]

    def side_by_side(k_part, m_part, live):
        pair = jnp.concatenate([k_part, m_part], 2)
        return jnp.where(live[:, None, None], pair, jnp.zeros_like(pair))

    def flat(blocks):
        return blocks.reshape(-1, node_size, node_size)

    def flipped(blocks):
        return jnp.swapaxes(flat(blocks), 1, 2)

    live_flat = link_live.reshape(-1)
    face_blocks = side_by_side(flat(k_iface), flat(m_iface), slot_live)
    local_blocks = jnp.concatenate(
        [
            side_by_side(k_diag, m_diag, jnp.ones((node_count,), bool)),
            side_by_side(flipped(k_link), flipped(m_link), live_flat),
            side_by_side(flat(k_link), flat(m_link), live_flat),
        ],
        0,
    )
    link_from = jnp.repeat(node_ids, link_slots)
    link_flat = link_to.reshape(-1)
    src_ids = jnp.concatenate([node_ids, link_flat, link_from])
    dst_ids = jnp.concatenate([node_ids, link_from, link_flat])
    tables = (local_blocks, src_ids, dst_ids, node_count)

    precond = 1.0 / jnp.diagonal(k_diag.astype(jnp.float32), axis1=1, axis2=2).reshape(-1)
    col_start = lax.axis_index(COLS) * col_part

    start = jnp.concatenate([x_start, p_start], 0)
    received = exchange(start, slot_ids, node_count)
    all_x, all_p = gather_cols(x_start, p_start)
    local = apply_local(start, tables)
    space = jnp.concatenate([all_x, all_p], 0)
    own, part = apply_faces(local, received, face_blocks, slot_ids, space, dof_count)
    own_kx, own_kp, own_mx, own_mp = [
        own[i * col_part : (i + 1) * col_part] for i in range(4)
    ]
    gram, (all_kx, all_mx) = reduce_gram(part, gather_cols(own_kx, own_mx))

    def block(gram, position):
        piece = gram[:, position * col_part : (position + 1) * col_part]
        return piece.reshape(modes, piece.shape[2])

    square = (modes, modes)
    pair = (2 * modes, 2 * modes)
    old_stiff = jnp.concatenate([block(gram, 0), block(gram, 1)], 0)
    old_mass = jnp.concatenate([block(gram, 2), block(gram, 3)], 0)
    (ritz_turned,) = dense(first_ritz_kernel, (square,), modes)(
        old_stiff[:modes, :modes], old_mass[:modes, :modes]
    )
    factors = dense(old_kernel, (pair,) * 3, modes)(old_stiff, old_mass)
    for step_index in range(STEPS):
        all_w = (all_kx - edot(ritz_turned, all_mx)) * precond[None, :]
        own_w = lax.dynamic_slice_in_dim(all_w, col_start, col_part, 0)
        received = exchange(own_w, slot_ids, node_count)
        local = apply_local(own_w, tables)
        if step_index == 0:
            own_kp, own_mp, own_w = lax.optimization_barrier((own_kp, own_mp, own_w))
            all_kp, all_mp = gather_cols(own_kp, own_mp)
        received, old_mass, factors, local, all_kp, all_mp = lax.optimization_barrier(
            (received, old_mass, factors, local, all_kp, all_mp)
        )
        space = jnp.concatenate([all_x, all_p, all_w], 0)
        own, part = apply_faces(local, received, face_blocks, slot_ids, space, dof_count)
        panels = []
        if step_index + 1 < STEPS:
            panels = gather_cols(own[:col_part], own[col_part:])
        gram, panels = reduce_gram(part, panels)
        stiff_w, mass_w = block(gram, 0), block(gram, 1)
        coeffs, ritz_turned = dense(ritz_kernel, ((modes, 3 * modes), square), modes)(
            stiff_w, mass_w, old_mass, *factors
        )
        if step_index + 1 == STEPS:
            mine = lax.dynamic_slice_in_dim(coeffs, col_start, col_part, 0)
            p_out = edot(mine[:, modes:], space[modes:])
            x_out = p_out + edot(mine[:, :modes], space[:modes])
            return (x_out, p_out, ritz_turned)
        all_kw, all_mw = panels
        wide_x = jnp.concatenate([all_kx, all_mx, all_x], 1)
        wide_rest = jnp.concatenate(
            [
                jnp.concatenate([all_kp, all_mp, all_p], 1),
                jnp.concatenate([all_kw, all_mw, all_w], 1),
            ],
            0,
        )
        new_p = edot(coeffs[:, modes:], wide_rest)
        new_x = new_p + edot(coeffs[:, :modes], wide_x)
        all_kx, all_mx, all_x = [new_x[:, i * row_count : (i + 1) * row_count] for i in range(3)]
        all_p = new_p[:, 2 * row_count :]
        old_mass, *factors = dense(carry_kernel, (pair,) * 4, modes)(
            coeffs, old_stiff, old_mass, stiff_w, mass_w
        )


def solution(mesh):
    rows, cols = mesh.devices.shape
    fine = Mesh(
        mesh.devices.reshape(rows // Y_SIZE, Y_SIZE, cols // CORES, CORES), ROWS + COLS
    )
    placed = (P(COLS, ROWS),) * 2 + (P(ROWS),) * 10
    return jax.shard_map(
        body,
        mesh=fine,
        in_specs=placed,
        out_specs=(P(COLS, ROWS), P(COLS, ROWS), P()),
        check_vma=False,
    )
```

```python
import functools

import jax
import jax.numpy as jnp
from jax import lax
from jax.experimental import pallas as pl
from jax.experimental.pallas import tpu as pltpu
from jax.sharding import Mesh, PartitionSpec as P

ROWS = ("z", "y")
COLS = ("x", "core")
Y_SIZE = 4
CORES = 2
STEPS = 2
RR_ITERS = 3
GROUP = 8


exact_dots = lax.Precision.HIGHEST


def edot(a, b):
    return jnp.dot(a, b, precision=exact_dots)


def swap(array, axis):
    return lax.all_to_all(array, axis, split_axis=0, concat_axis=0, tiled=True)


def spread(array, axis):
    count = lax.axis_size(axis)
    return swap(jnp.broadcast_to(array[None], (count,) + array.shape), axis)


def gather_cols(*blocks):
    count = blocks[0].shape[0]
    moved = lax.all_gather(jnp.concatenate(blocks, 0), COLS, axis=0)
    return [
        moved[:, i * count : (i + 1) * count].reshape(-1, blocks[0].shape[1])
        for i in range(len(blocks))
    ]


def reduce_gram(part, beside):
    piece = jnp.sum(swap(part.reshape(lax.axis_size("y"), -1), "y"), 0)
    piece = jnp.sum(spread(piece, "z"), 0)
    piece, beside = lax.optimization_barrier((piece, beside))
    whole = spread(piece, ("y",) + COLS)
    whole = whole.reshape(lax.axis_size("y"), lax.axis_size(COLS), -1, part.shape[1])
    return jnp.swapaxes(whole, 0, 1).reshape((-1,) + part.shape), beside


def nn(a, b):
    return lax.dot_general(
        a, b, (((1,), (0,)), ((), ())), precision=exact_dots, preferred_element_type=jnp.float32
    )


def nt(a, b):
    return lax.dot_general(
        a, b, (((1,), (1,)), ((), ())), precision=exact_dots, preferred_element_type=jnp.float32
    )


def node_rows(vec_ref, node_ref):
    half = vec_ref.shape[0] // 2
    size = vec_ref.shape[1] // node_ref.shape[0]
    for s in range(node_ref.shape[0]):
        both = [vec_ref[h * half : (h + 1) * half, s * size : (s + 1) * size] for h in range(2)]
        node_ref[s] = jnp.concatenate(both, 1)


def pick_kernel(slot_ref, vec_ref, out_ref, node_ref):
    node_rows(vec_ref, node_ref)
    rows = node_ref.shape[1]

    def group(g, carry):
        first = pl.multiple_of(g * (rows * GROUP), 8)
        pieces = [node_ref[slot_ref[g * GROUP + i]] for i in range(GROUP)]
        out_ref[pl.ds(first, rows * GROUP), :] = jnp.concatenate(pieces, 0)
        return carry

    lax.fori_loop(0, out_ref.shape[0] // (rows * GROUP), group, 0, unroll=2)


def add_product(acc_ref, node, piece, block):
    rows, lanes = piece.shape
    padded = acc_ref.shape[1] // 2
    fill = jnp.zeros((padded - rows, lanes), jnp.float32)
    full = jnp.concatenate([piece, fill], 0)
    half = lanes // 2
    pair = jnp.concatenate([full, pltpu.roll(full, half, 1)], 0)[:, :half]
    high = pair.astype(jnp.bfloat16)
    rest = pair - high.astype(jnp.float32)
    middle = rest.astype(jnp.bfloat16)
    low = (rest - middle.astype(jnp.float32)).astype(jnp.bfloat16)
    terms = jnp.concatenate([high, middle, low], 0)
    out = jnp.dot(terms, block, preferred_element_type=jnp.float32)
    two = 2 * padded
    acc_ref[node] = acc_ref[node] + (out[:two] + out[two : 2 * two] + out[2 * two :])


def start_blocks(first, hbm_ref, blocks_ref, sems):
    chunks = sems.shape[0]
    size = blocks_ref.shape[0] // chunks
    copies = []
    for c in range(chunks):
        source = hbm_ref.at[pl.ds(first + c * size, size)]
        target = blocks_ref.at[pl.ds(c * size, size)]
        copies.append(pltpu.make_async_copy(source, target, sems.at[c]))
        copies[c].start()
    return copies, size


def local_kernel(dst_ref, src_ref, vec_ref, hbm_ref, acc_ref, node_ref, blocks_ref, sems):
    first = hbm_ref.shape[0] - blocks_ref.shape[0]
    copies, size = start_blocks(first, hbm_ref, blocks_ref, sems)
    node_rows(vec_ref, node_ref)
    acc_ref[...] = jnp.zeros(acc_ref.shape, jnp.float32)

    def group(g, carry):
        for i in range(GROUP):
            k = g * GROUP + i
            add_product(acc_ref, dst_ref[k], node_ref[src_ref[k]], blocks_ref[k])
        return carry

    for c, copy in enumerate(copies):
        copy.wait()
        lax.fori_loop(c * size // GROUP, (c + 1) * size // GROUP, group, 0)


def face_kernel(
    dof_count,
    dst_ref,
    recv_ref,
    start_ref,
    hbm_ref,
    space_ref,
    own_ref,
    part_ref,
    acc_ref,
    blocks_ref,
    sems,
):
    copies, count = start_blocks(0, hbm_ref, blocks_ref, sems)
    slots = dst_ref.shape[0]
    rows = recv_ref.shape[0] // slots
    nodes, two, lanes = acc_ref.shape
    padded = two // 2
    size = lanes // 2
    acc_ref[...] = start_ref[...]

    def group(g, carry):
        first = pl.multiple_of(g * (rows * GROUP), 8)
        chunk = recv_ref[pl.ds(first, rows * GROUP), :]
        for i in range(GROUP):
            k = g * GROUP + i
            add_product(acc_ref, dst_ref[k], chunk[rows * i : rows * (i + 1)], blocks_ref[k])
        return carry

    for c, copy in enumerate(copies):
        copy.wait()
        lax.fori_loop(c * count // GROUP, (c + 1) * count // GROUP, group, 0)
    for which in range(2):
        for h in range(2):
            row = which * 2 * rows + h * rows
            for s in range(nodes):
                own_ref[row : row + rows, s * size : (s + 1) * size] = acc_ref[
                    s, h * padded : h * padded + rows, which * size : (which + 1) * size
                ]
    part_ref[...] = nt(own_ref[...], space_ref[...]) / dof_count


def at(*spaces):
    return [pl.BlockSpec(memory_space=space) for space in spaces]


def exchange(vectors, slot_ids, node_count):
    rows = vectors.shape[0] // 2
    lanes = 2 * vectors.shape[1] // node_count
    picked = pl.pallas_call(
        pick_kernel,
        out_shape=jax.ShapeDtypeStruct((slot_ids.shape[0] * rows, lanes), jnp.float32),
        in_specs=at(pltpu.SMEM, pltpu.VMEM),
        out_specs=at(pltpu.VMEM)[0],
        scratch_shapes=[pltpu.VMEM((node_count, rows, lanes), jnp.float32)],
    )(slot_ids, vectors)
    owners = lax.axis_size(ROWS)
    return swap(picked.reshape(owners, -1), ROWS).reshape(picked.shape)


def apply_local(vectors, tables):
    blocks, src_ids, dst_ids, node_count = tables
    col_count, row_count = vectors.shape
    rows = col_count // 2
    lanes = 2 * row_count // node_count
    padded = -(-rows // 8) * 8
    return pl.pallas_call(
        local_kernel,
        out_shape=jax.ShapeDtypeStruct((node_count, 2 * padded, lanes), jnp.float32),
        in_specs=at(pltpu.SMEM, pltpu.SMEM, pltpu.VMEM, pltpu.HBM),
        out_specs=at(pltpu.VMEM)[0],
        scratch_shapes=[
            pltpu.VMEM((node_count, rows, lanes), jnp.float32),
            pltpu.VMEM(src_ids.shape + blocks.shape[1:], blocks.dtype),
            pltpu.SemaphoreType.DMA((1,)),
        ],
        compiler_params=pltpu.CompilerParams(vmem_limit_bytes=60 * 2**20),
    )(dst_ids, src_ids, vectors, blocks)


def apply_faces(local, received, blocks, slot_ids, space, dof_count):
    col_count = 2 * received.shape[0] // slot_ids.shape[0]
    shapes = ((2 * col_count, space.shape[1]), (2 * col_count, space.shape[0]))
    return pl.pallas_call(
        functools.partial(face_kernel, dof_count),
        out_shape=tuple(jax.ShapeDtypeStruct(s, jnp.float32) for s in shapes),
        in_specs=at(pltpu.SMEM, pltpu.VMEM, pltpu.VMEM, pltpu.HBM, pltpu.VMEM),
        out_specs=at(pltpu.VMEM, pltpu.VMEM),
        scratch_shapes=[
            pltpu.VMEM(local.shape, jnp.float32),
            pltpu.VMEM(slot_ids.shape + blocks.shape[1:], blocks.dtype),
            pltpu.SemaphoreType.DMA((4,)),
        ],
        compiler_params=pltpu.CompilerParams(vmem_limit_bytes=60 * 2**20),
    )(slot_ids, received, local, blocks, space)


LANES = 128
PANEL = 8

def lower_inverse(matrix, out_ref):
    size = matrix.shape[0]
    tiles = size // PANEL
    wide = jnp.concatenate([matrix, jnp.zeros((size, LANES - size), jnp.float32)], 1)
    row = lax.broadcasted_iota(jnp.int32, (size, LANES), 0)
    lane = lax.broadcasted_iota(jnp.int32, (size, LANES), 1)
    ident = jnp.where(row == lane, 1.0, 0.0).astype(jnp.float32)
    left = [wide[PANEL * t : PANEL * t + PANEL] for t in range(tiles)]
    right = [ident[PANEL * t : PANEL * t + PANEL] for t in range(tiles)]
    full = (PANEL, LANES)

    def lane_splat(tile, k):
        return jnp.broadcast_to(tile[:, k : k + 1], full)

    def row_splat(tile, i):
        return jnp.broadcast_to(tile[i : i + 1, :], full)

    for p in range(tiles):
        base = PANEL * p
        cols = [lane_splat(left[p], base + k) for k in range(PANEL)]
        s = {(i, k): row_splat(cols[k], i) for k in range(PANEL) for i in range(k, PANEL)}
        rows_l = [row_splat(left[p], i) for i in range(PANEL)]
        rows_r = [row_splat(right[p], i) for i in range(PANEL)]
        later = range(p + 1, min(p + 2, tiles))
        below = {t: [lane_splat(left[t], base + k) for k in range(PANEL)] for t in later}
        lows, roots, outs = [], [], []
        for k in range(PANEL):
            r = lax.rsqrt(s[k, k])
            low = {i: s[i, k] * r for i in range(k + 1, PANEL)}
            for m in range(k + 1, PANEL):
                for i in range(m, PANEL):
                    s[i, m] = s[i, m] - low[i] * low[m]
            new_l = rows_l[k] * r
            new_r = rows_r[k] * r
            out_ref[base + k : base + k + 1, :] = new_r[0:1, :size]
            for i in range(k + 1, PANEL):
                rows_l[i] = rows_l[i] - low[i] * new_l
                rows_r[i] = rows_r[i] - low[i] * new_r
            for t in later:
                factor = below[t][k] * r
                for i in range(k + 1, PANEL):
                    below[t][i] = below[t][i] - low[i] * factor
                left[t] = left[t] - factor * new_l
                right[t] = right[t] - factor * new_r
            lows.append(low)
            roots.append(r)
            outs.append((new_l, new_r))
        for t in range(p + 2, tiles):
            factors = [lane_splat(left[t], base + k) for k in range(PANEL)]
            for k in range(PANEL):
                factors[k] = factors[k] * roots[k]
                for i in range(k + 1, PANEL):
                    factors[i] = factors[i] - lows[k][i] * factors[k]
                left[t] = left[t] - factors[k] * outs[k][0]
                right[t] = right[t] - factors[k] * outs[k][1]


def first_ritz_kernel(stiff_ref, mass_ref, ritz_ref, tmp_ref):
    lower_inverse(mass_ref[...], tmp_ref)
    inv = tmp_ref[...]
    ritz_ref[...] = nn(nt(stiff_ref[...], inv), inv)


def factor_old(stiff, mass, j_ref, jm_ref, b_ref, tmp_ref):
    n = tmp_ref.shape[0]
    lower_inverse(stiff[:n, :n], tmp_ref)
    first = tmp_ref[...]
    q = nt(stiff[n:, :n], first)
    lower_inverse(stiff[n:, n:] - nt(q, q), tmp_ref)
    second = tmp_ref[...]
    j_ref[:n, :n] = first
    j_ref[:n, n:] = jnp.zeros((n, n), jnp.float32)
    j_ref[n:, :n] = -nn(second, nn(q, first))
    j_ref[n:, n:] = second
    j = j_ref[...]
    jm = nt(mass, j)
    jm_ref[...] = jm
    b_ref[...] = nn(j, jm)


def old_kernel(stiff_ref, mass_ref, j_ref, jm_ref, b_ref, tmp_ref):
    factor_old(stiff_ref[...], mass_ref[...], j_ref, jm_ref, b_ref, tmp_ref)


def carry_kernel(
    y_ref, gxp_ref, mxp_ref, gw_ref, mw_ref, next_ref, j_ref, jm_ref, b_ref, tmp_ref
):
    n = tmp_ref.shape[0]
    ya = y_ref[:, : 2 * n]
    yb = y_ref[:, 2 * n :]
    lane = lax.broadcasted_iota(jnp.int32, ya.shape, 1)
    pa = jnp.concatenate([ya, jnp.where(lane < n, 0.0, ya)], 0)
    pb = jnp.concatenate([yb, yb], 0)

    def turned(old_ref, col_ref):
        col = col_ref[:, : 2 * n]
        ha = nn(pa, old_ref[...]) + nn(pb, col)
        hb = nt(pa, col) + nn(pb, col_ref[:, 2 * n :])
        return nt(ha, pa) + nt(hb, pb)

    mass = turned(mxp_ref, mw_ref)
    next_ref[...] = mass
    factor_old(turned(gxp_ref, gw_ref), mass, j_ref, jm_ref, b_ref, tmp_ref)


def ritz_kernel(
    gw_ref, mw_ref, mxp_ref, j_ref, jm_ref, b_ref, y_ref, ritz_ref, tmp_ref
):
    n = tmp_ref.shape[0]
    j = j_ref[...]
    bxx = b_ref[...]
    qt = nt(gw_ref[:, : 2 * n], j)
    lower_inverse(gw_ref[:, 2 * n :] - nt(qt, qt), tmp_ref)
    lw = tmp_ref[...]
    t = nn(qt, j)
    mwx = mw_ref[:, : 2 * n]
    d = mwx - nn(t, mxp_ref[...])
    e = mw_ref[:, 2 * n :] - nt(t, mwx) - nt(d, t)
    bwx = nn(lw, nt(d, j))
    bww = nt(nn(lw, e), lw)
    va = jm_ref[:n, :]
    vb = jnp.transpose(nn(lw, d[:, :n]))
    ua = ub = None
    for inner_index in range(RR_ITERS):
        wa = nn(va, bxx) + nn(vb, bwx)
        wb = nt(va, bwx) + nn(vb, bww)
        lower_inverse(nt(wa, va) + nt(wb, vb), tmp_ref)
        lc = tmp_ref[...]
        ua, ub = nn(lc, va), nn(lc, vb)
        va, vb = nn(lc, wa), nn(lc, wb)
    ritz_ref[...] = nt(ua, ua) + nt(ub, ub)
    yw = nn(ub, lw)
    y_ref[:, : 2 * n] = nn(ua, j) - nn(yw, t)
    y_ref[:, 2 * n :] = yw


def dense(kernel, shapes, size):
    return pl.pallas_call(
        kernel,
        out_shape=tuple(jax.ShapeDtypeStruct(s, jnp.float32) for s in shapes),
        scratch_shapes=[pltpu.VMEM((size, size), jnp.float32)],
    )


def body(
    x_start,
    p_start,
    k_diag,
    k_link,
    m_diag,
    m_link,
    link_to,
    link_count,
    k_iface,
    m_iface,
    iface_local,
    iface_live,
):
    col_part, row_count = x_start.shape
    modes = col_part * lax.axis_size(COLS)
    dof_count = row_count * lax.axis_size(ROWS)
    node_count, link_slots = link_to.shape
    node_size = k_diag.shape[1]
    node_ids = jnp.arange(node_count, dtype=jnp.int32)
    slot_ids = iface_local.reshape(-1)
    slot_live = iface_live.reshape(-1) > 0
    link_live = jnp.arange(link_slots, dtype=jnp.int32)[None, :] < link_count[:, None]

    def side_by_side(k_part, m_part, live):
        pair = jnp.concatenate([k_part, m_part], 2)
        return jnp.where(live[:, None, None], pair, jnp.zeros_like(pair))

    def flat(blocks):
        return blocks.reshape(-1, node_size, node_size)

    def flipped(blocks):
        return jnp.swapaxes(flat(blocks), 1, 2)

    live_flat = link_live.reshape(-1)
    blocks = jnp.concatenate(
        [
            side_by_side(flat(k_iface), flat(m_iface), slot_live),
            side_by_side(k_diag, m_diag, jnp.ones((node_count,), bool)),
            side_by_side(flipped(k_link), flipped(m_link), live_flat),
            side_by_side(flat(k_link), flat(m_link), live_flat),
        ],
        0,
    )
    link_from = jnp.repeat(node_ids, link_slots)
    link_flat = link_to.reshape(-1)
    src_ids = jnp.concatenate([node_ids, link_flat, link_from])
    dst_ids = jnp.concatenate([node_ids, link_from, link_flat])
    tables = (blocks, src_ids, dst_ids, node_count)

    precond = 1.0 / jnp.diagonal(k_diag.astype(jnp.float32), axis1=1, axis2=2).reshape(-1)
    col_start = lax.axis_index(COLS) * col_part

    start = jnp.concatenate([x_start, p_start], 0)
    received = exchange(start, slot_ids, node_count)
    all_x, all_p = gather_cols(x_start, p_start)
    local = apply_local(start, tables)
    space = jnp.concatenate([all_x, all_p], 0)
    own, part = apply_faces(local, received, blocks, slot_ids, space, dof_count)
    own_kx, own_kp, own_mx, own_mp = [
        own[i * col_part : (i + 1) * col_part] for i in range(4)
    ]
    gram, (all_kx, all_mx) = reduce_gram(part, gather_cols(own_kx, own_mx))

    def block(gram, position):
        piece = gram[:, position * col_part : (position + 1) * col_part]
        return piece.reshape(modes, piece.shape[2])

    square = (modes, modes)
    pair = (2 * modes, 2 * modes)
    old_stiff = jnp.concatenate([block(gram, 0), block(gram, 1)], 0)
    old_mass = jnp.concatenate([block(gram, 2), block(gram, 3)], 0)
    (ritz_turned,) = dense(first_ritz_kernel, (square,), modes)(
        old_stiff[:modes, :modes], old_mass[:modes, :modes]
    )
    factors = dense(old_kernel, (pair,) * 3, modes)(old_stiff, old_mass)
    for step_index in range(STEPS):
        all_w = (all_kx - edot(ritz_turned, all_mx)) * precond[None, :]
        own_w = lax.dynamic_slice_in_dim(all_w, col_start, col_part, 0)
        received = exchange(own_w, slot_ids, node_count)
        local = apply_local(own_w, tables)
        if step_index == 0:
            own_kp, own_mp, own_w = lax.optimization_barrier((own_kp, own_mp, own_w))
            all_kp, all_mp = gather_cols(own_kp, own_mp)
        received, old_mass, factors, local, all_kp, all_mp = lax.optimization_barrier(
            (received, old_mass, factors, local, all_kp, all_mp)
        )
        space = jnp.concatenate([all_x, all_p, all_w], 0)
        own, part = apply_faces(local, received, blocks, slot_ids, space, dof_count)
        panels = []
        if step_index + 1 < STEPS:
            panels = gather_cols(own[:col_part], own[col_part:])
        gram, panels = reduce_gram(part, panels)
        stiff_w, mass_w = block(gram, 0), block(gram, 1)
        coeffs, ritz_turned = dense(ritz_kernel, ((modes, 3 * modes), square), modes)(
            stiff_w, mass_w, old_mass, *factors
        )
        if step_index + 1 == STEPS:
            mine = lax.dynamic_slice_in_dim(coeffs, col_start, col_part, 0)
            p_out = edot(mine[:, modes:], space[modes:])
            x_out = p_out + edot(mine[:, :modes], space[:modes])
            return (x_out, p_out, ritz_turned)
        all_kw, all_mw = panels
        wide_x = jnp.concatenate([all_kx, all_mx, all_x], 1)
        wide_rest = jnp.concatenate(
            [
                jnp.concatenate([all_kp, all_mp, all_p], 1),
                jnp.concatenate([all_kw, all_mw, all_w], 1),
            ],
            0,
        )
        new_p = edot(coeffs[:, modes:], wide_rest)
        new_x = new_p + edot(coeffs[:, :modes], wide_x)
        all_kx, all_mx, all_x = [new_x[:, i * row_count : (i + 1) * row_count] for i in range(3)]
        all_p = new_p[:, 2 * row_count :]
        old_mass, *factors = dense(carry_kernel, (pair,) * 4, modes)(
            coeffs, old_stiff, old_mass, stiff_w, mass_w
        )


def solution(mesh):
    rows, cols = mesh.devices.shape
    fine = Mesh(
        mesh.devices.reshape(rows // Y_SIZE, Y_SIZE, cols // CORES, CORES), ROWS + COLS
    )
    placed = (P(COLS, ROWS),) * 2 + (P(ROWS),) * 10
    return jax.shard_map(
        body,
        mesh=fine,
        in_specs=placed,
        out_specs=(P(COLS, ROWS), P(COLS, ROWS), P()),
        check_vma=False,
    )
```

```python
import functools

import jax
import jax.numpy as jnp
from jax import lax
from jax.experimental import pallas as pl
from jax.experimental.pallas import tpu as pltpu
from jax.sharding import Mesh, PartitionSpec as P

ROWS = ("z", "y")
COLS = ("x", "core")
Y_SIZE = 4
CORES = 2
STEPS = 2
RR_ITERS = 3
GROUP = 8


exact_dots = lax.Precision.HIGHEST


def edot(a, b):
    return jnp.dot(a, b, precision=exact_dots)


def swap(array, axis):
    return lax.all_to_all(array, axis, split_axis=0, concat_axis=0, tiled=True)


def spread(array, axis):
    count = lax.axis_size(axis)
    return swap(jnp.broadcast_to(array[None], (count,) + array.shape), axis)


def gather_cols(*blocks):
    count = blocks[0].shape[0]
    moved = lax.all_gather(jnp.concatenate(blocks, 0), COLS, axis=0)
    return [
        moved[:, i * count : (i + 1) * count].reshape(-1, blocks[0].shape[1])
        for i in range(len(blocks))
    ]


def reduce_gram(part):
    piece = jnp.sum(swap(part.reshape(lax.axis_size("y"), -1), "y"), 0)
    piece = jnp.sum(spread(piece, "z"), 0)
    whole = spread(piece, ("y",) + COLS)
    whole = whole.reshape(lax.axis_size("y"), lax.axis_size(COLS), -1, part.shape[1])
    return jnp.swapaxes(whole, 0, 1).reshape((-1,) + part.shape)


def nn(a, b):
    return lax.dot_general(
        a, b, (((1,), (0,)), ((), ())), precision=exact_dots, preferred_element_type=jnp.float32
    )


def nt(a, b):
    return lax.dot_general(
        a, b, (((1,), (1,)), ((), ())), precision=exact_dots, preferred_element_type=jnp.float32
    )


def node_rows(vec_ref, node_ref):
    half = vec_ref.shape[0] // 2
    size = vec_ref.shape[1] // node_ref.shape[0]
    for s in range(node_ref.shape[0]):
        both = [vec_ref[h * half : (h + 1) * half, s * size : (s + 1) * size] for h in range(2)]
        node_ref[s] = jnp.concatenate(both, 1)


def pick_kernel(slot_ref, vec_ref, out_ref, node_ref):
    node_rows(vec_ref, node_ref)
    rows = node_ref.shape[1]

    def group(g, carry):
        first = pl.multiple_of(g * (rows * GROUP), 8)
        pieces = [node_ref[slot_ref[g * GROUP + i]] for i in range(GROUP)]
        out_ref[pl.ds(first, rows * GROUP), :] = jnp.concatenate(pieces, 0)
        return carry

    lax.fori_loop(0, out_ref.shape[0] // (rows * GROUP), group, 0, unroll=2)


def add_product(acc_ref, node, piece, block):
    rows, lanes = piece.shape
    padded = acc_ref.shape[1] // 2
    fill = jnp.zeros((padded - rows, lanes), jnp.float32)
    full = jnp.concatenate([piece, fill], 0)
    half = lanes // 2
    pair = jnp.concatenate([full, pltpu.roll(full, half, 1)], 0)[:, :half]
    high = pair.astype(jnp.bfloat16)
    rest = pair - high.astype(jnp.float32)
    middle = rest.astype(jnp.bfloat16)
    low = (rest - middle.astype(jnp.float32)).astype(jnp.bfloat16)
    terms = jnp.concatenate([high, middle, low], 0)
    out = jnp.dot(terms, block, preferred_element_type=jnp.float32)
    two = 2 * padded
    acc_ref[node] = acc_ref[node] + (out[:two] + out[two : 2 * two] + out[2 * two :])


def local_kernel(dst_ref, src_ref, vec_ref, blocks_ref, acc_ref, node_ref):
    node_rows(vec_ref, node_ref)
    acc_ref[...] = jnp.zeros(acc_ref.shape, jnp.float32)
    first = blocks_ref.shape[0] - src_ref.shape[0]

    def group(g, carry):
        for i in range(GROUP):
            k = g * GROUP + i
            add_product(acc_ref, dst_ref[k], node_ref[src_ref[k]], blocks_ref[first + k])
        return carry

    lax.fori_loop(0, src_ref.shape[0] // GROUP, group, 0)


def face_kernel(
    dof_count, dst_ref, recv_ref, start_ref, blocks_ref, space_ref, own_ref, part_ref, acc_ref
):
    slots = dst_ref.shape[0]
    rows = recv_ref.shape[0] // slots
    nodes, two, lanes = acc_ref.shape
    padded = two // 2
    size = lanes // 2
    acc_ref[...] = start_ref[...]

    def group(g, carry):
        first = pl.multiple_of(g * (rows * GROUP), 8)
        chunk = recv_ref[pl.ds(first, rows * GROUP), :]
        for i in range(GROUP):
            k = g * GROUP + i
            add_product(acc_ref, dst_ref[k], chunk[rows * i : rows * (i + 1)], blocks_ref[k])
        return carry

    lax.fori_loop(0, slots // GROUP, group, 0)
    for which in range(2):
        for h in range(2):
            row = which * 2 * rows + h * rows
            for s in range(nodes):
                own_ref[row : row + rows, s * size : (s + 1) * size] = acc_ref[
                    s, h * padded : h * padded + rows, which * size : (which + 1) * size
                ]
    part_ref[...] = nt(own_ref[...], space_ref[...]) / dof_count


def at(*spaces):
    return [pl.BlockSpec(memory_space=space) for space in spaces]


def exchange(vectors, slot_ids, node_count):
    rows = vectors.shape[0] // 2
    lanes = 2 * vectors.shape[1] // node_count
    picked = pl.pallas_call(
        pick_kernel,
        out_shape=jax.ShapeDtypeStruct((slot_ids.shape[0] * rows, lanes), jnp.float32),
        in_specs=at(pltpu.SMEM, pltpu.VMEM),
        out_specs=at(pltpu.VMEM)[0],
        scratch_shapes=[pltpu.VMEM((node_count, rows, lanes), jnp.float32)],
    )(slot_ids, vectors)
    owners = lax.axis_size(ROWS)
    return swap(picked.reshape(owners, -1), ROWS).reshape(picked.shape)


def apply_local(vectors, tables):
    blocks, src_ids, dst_ids, node_count = tables
    col_count, row_count = vectors.shape
    rows = col_count // 2
    lanes = 2 * row_count // node_count
    padded = -(-rows // 8) * 8
    return pl.pallas_call(
        local_kernel,
        out_shape=jax.ShapeDtypeStruct((node_count, 2 * padded, lanes), jnp.float32),
        in_specs=at(pltpu.SMEM, pltpu.SMEM, pltpu.VMEM, pltpu.VMEM),
        out_specs=at(pltpu.VMEM)[0],
        scratch_shapes=[pltpu.VMEM((node_count, rows, lanes), jnp.float32)],
        compiler_params=pltpu.CompilerParams(vmem_limit_bytes=40 * 2**20),
    )(dst_ids, src_ids, vectors, blocks)


def apply_faces(local, received, blocks, slot_ids, space, dof_count):
    col_count = 2 * received.shape[0] // slot_ids.shape[0]
    shapes = ((2 * col_count, space.shape[1]), (2 * col_count, space.shape[0]))
    return pl.pallas_call(
        functools.partial(face_kernel, dof_count),
        out_shape=tuple(jax.ShapeDtypeStruct(s, jnp.float32) for s in shapes),
        in_specs=at(pltpu.SMEM, *(pltpu.VMEM,) * 4),
        out_specs=at(pltpu.VMEM, pltpu.VMEM),
        scratch_shapes=[pltpu.VMEM(local.shape, jnp.float32)],
        compiler_params=pltpu.CompilerParams(vmem_limit_bytes=40 * 2**20),
    )(slot_ids, received, local, blocks, space)


LANES = 128
PANEL = 8

def lower_inverse(matrix, out_ref):
    size = matrix.shape[0]
    tiles = size // PANEL
    wide = jnp.concatenate([matrix, jnp.zeros((size, LANES - size), jnp.float32)], 1)
    row = lax.broadcasted_iota(jnp.int32, (size, LANES), 0)
    lane = lax.broadcasted_iota(jnp.int32, (size, LANES), 1)
    ident = jnp.where(row == lane, 1.0, 0.0).astype(jnp.float32)
    left = [wide[PANEL * t : PANEL * t + PANEL] for t in range(tiles)]
    right = [ident[PANEL * t : PANEL * t + PANEL] for t in range(tiles)]
    full = (PANEL, LANES)

    def lane_splat(tile, k):
        return jnp.broadcast_to(tile[:, k : k + 1], full)

    def row_splat(tile, i):
        return jnp.broadcast_to(tile[i : i + 1, :], full)

    for p in range(tiles):
        base = PANEL * p
        cols = [lane_splat(left[p], base + k) for k in range(PANEL)]
        s = {(i, k): row_splat(cols[k], i) for k in range(PANEL) for i in range(k, PANEL)}
        rows_l = [row_splat(left[p], i) for i in range(PANEL)]
        rows_r = [row_splat(right[p], i) for i in range(PANEL)]
        later = range(p + 1, min(p + 2, tiles))
        below = {t: [lane_splat(left[t], base + k) for k in range(PANEL)] for t in later}
        lows, roots, outs = [], [], []
        for k in range(PANEL):
            r = lax.rsqrt(s[k, k])
            low = {i: s[i, k] * r for i in range(k + 1, PANEL)}
            for m in range(k + 1, PANEL):
                for i in range(m, PANEL):
                    s[i, m] = s[i, m] - low[i] * low[m]
            new_l = rows_l[k] * r
            new_r = rows_r[k] * r
            out_ref[base + k : base + k + 1, :] = new_r[0:1, :size]
            for i in range(k + 1, PANEL):
                rows_l[i] = rows_l[i] - low[i] * new_l
                rows_r[i] = rows_r[i] - low[i] * new_r
            for t in later:
                factor = below[t][k] * r
                for i in range(k + 1, PANEL):
                    below[t][i] = below[t][i] - low[i] * factor
                left[t] = left[t] - factor * new_l
                right[t] = right[t] - factor * new_r
            lows.append(low)
            roots.append(r)
            outs.append((new_l, new_r))
        for t in range(p + 2, tiles):
            factors = [lane_splat(left[t], base + k) for k in range(PANEL)]
            for k in range(PANEL):
                factors[k] = factors[k] * roots[k]
                for i in range(k + 1, PANEL):
                    factors[i] = factors[i] - lows[k][i] * factors[k]
                left[t] = left[t] - factors[k] * outs[k][0]
                right[t] = right[t] - factors[k] * outs[k][1]


def first_ritz_kernel(stiff_ref, mass_ref, ritz_ref, tmp_ref):
    lower_inverse(mass_ref[...], tmp_ref)
    inv = tmp_ref[...]
    ritz_ref[...] = nn(nt(stiff_ref[...], inv), inv)


def factor_old(stiff, mass, j_ref, jm_ref, b_ref, tmp_ref):
    n = tmp_ref.shape[0]
    lower_inverse(stiff[:n, :n], tmp_ref)
    first = tmp_ref[...]
    q = nt(stiff[n:, :n], first)
    lower_inverse(stiff[n:, n:] - nt(q, q), tmp_ref)
    second = tmp_ref[...]
    j_ref[:n, :n] = first
    j_ref[:n, n:] = jnp.zeros((n, n), jnp.float32)
    j_ref[n:, :n] = -nn(second, nn(q, first))
    j_ref[n:, n:] = second
    j = j_ref[...]
    jm = nt(mass, j)
    jm_ref[...] = jm
    b_ref[...] = nn(j, jm)


def old_kernel(stiff_ref, mass_ref, j_ref, jm_ref, b_ref, tmp_ref):
    factor_old(stiff_ref[...], mass_ref[...], j_ref, jm_ref, b_ref, tmp_ref)


def carry_kernel(
    y_ref, gxp_ref, mxp_ref, gw_ref, mw_ref, next_ref, j_ref, jm_ref, b_ref, tmp_ref
):
    n = tmp_ref.shape[0]
    ya = y_ref[:, : 2 * n]
    yb = y_ref[:, 2 * n :]
    lane = lax.broadcasted_iota(jnp.int32, ya.shape, 1)
    pa = jnp.concatenate([ya, jnp.where(lane < n, 0.0, ya)], 0)
    pb = jnp.concatenate([yb, yb], 0)

    def turned(old_ref, col_ref):
        col = col_ref[:, : 2 * n]
        ha = nn(pa, old_ref[...]) + nn(pb, col)
        hb = nt(pa, col) + nn(pb, col_ref[:, 2 * n :])
        return nt(ha, pa) + nt(hb, pb)

    mass = turned(mxp_ref, mw_ref)
    next_ref[...] = mass
    factor_old(turned(gxp_ref, gw_ref), mass, j_ref, jm_ref, b_ref, tmp_ref)


def ritz_kernel(
    gw_ref, mw_ref, mxp_ref, j_ref, jm_ref, b_ref, y_ref, ritz_ref, tmp_ref
):
    n = tmp_ref.shape[0]
    j = j_ref[...]
    bxx = b_ref[...]
    qt = nt(gw_ref[:, : 2 * n], j)
    lower_inverse(gw_ref[:, 2 * n :] - nt(qt, qt), tmp_ref)
    lw = tmp_ref[...]
    t = nn(qt, j)
    mwx = mw_ref[:, : 2 * n]
    d = mwx - nn(t, mxp_ref[...])
    e = mw_ref[:, 2 * n :] - nt(t, mwx) - nt(d, t)
    bwx = nn(lw, nt(d, j))
    bww = nt(nn(lw, e), lw)
    va = jm_ref[:n, :]
    vb = jnp.transpose(nn(lw, d[:, :n]))
    ua = ub = None
    for inner_index in range(RR_ITERS):
        wa = nn(va, bxx) + nn(vb, bwx)
        wb = nt(va, bwx) + nn(vb, bww)
        lower_inverse(nt(wa, va) + nt(wb, vb), tmp_ref)
        lc = tmp_ref[...]
        ua, ub = nn(lc, va), nn(lc, vb)
        va, vb = nn(lc, wa), nn(lc, wb)
    ritz_ref[...] = nt(ua, ua) + nt(ub, ub)
    yw = nn(ub, lw)
    y_ref[:, : 2 * n] = nn(ua, j) - nn(yw, t)
    y_ref[:, 2 * n :] = yw


def dense(kernel, shapes, size):
    return pl.pallas_call(
        kernel,
        out_shape=tuple(jax.ShapeDtypeStruct(s, jnp.float32) for s in shapes),
        scratch_shapes=[pltpu.VMEM((size, size), jnp.float32)],
    )


def body(
    x_start,
    p_start,
    k_diag,
    k_link,
    m_diag,
    m_link,
    link_to,
    link_count,
    k_iface,
    m_iface,
    iface_local,
    iface_live,
):
    col_part, row_count = x_start.shape
    modes = col_part * lax.axis_size(COLS)
    dof_count = row_count * lax.axis_size(ROWS)
    node_count, link_slots = link_to.shape
    node_size = k_diag.shape[1]
    node_ids = jnp.arange(node_count, dtype=jnp.int32)
    slot_ids = iface_local.reshape(-1)
    slot_live = iface_live.reshape(-1) > 0
    link_live = jnp.arange(link_slots, dtype=jnp.int32)[None, :] < link_count[:, None]

    def side_by_side(k_part, m_part, live):
        pair = jnp.concatenate([k_part, m_part], 2)
        return jnp.where(live[:, None, None], pair, jnp.zeros_like(pair))

    def flat(blocks):
        return blocks.reshape(-1, node_size, node_size)

    def flipped(blocks):
        return jnp.swapaxes(flat(blocks), 1, 2)

    live_flat = link_live.reshape(-1)
    blocks = jnp.concatenate(
        [
            side_by_side(flat(k_iface), flat(m_iface), slot_live),
            side_by_side(k_diag, m_diag, jnp.ones((node_count,), bool)),
            side_by_side(flipped(k_link), flipped(m_link), live_flat),
            side_by_side(flat(k_link), flat(m_link), live_flat),
        ],
        0,
    )
    link_from = jnp.repeat(node_ids, link_slots)
    link_flat = link_to.reshape(-1)
    src_ids = jnp.concatenate([node_ids, link_flat, link_from])
    dst_ids = jnp.concatenate([node_ids, link_from, link_flat])
    tables = (blocks, src_ids, dst_ids, node_count)

    precond = 1.0 / jnp.diagonal(k_diag.astype(jnp.float32), axis1=1, axis2=2).reshape(-1)
    col_start = lax.axis_index(COLS) * col_part

    start = jnp.concatenate([x_start, p_start], 0)
    received = exchange(start, slot_ids, node_count)
    all_x, all_p = gather_cols(x_start, p_start)
    local = apply_local(start, tables)
    space = jnp.concatenate([all_x, all_p], 0)
    own, part = apply_faces(local, received, blocks, slot_ids, space, dof_count)
    gram = reduce_gram(part)
    all_kx, all_kp, all_mx, all_mp = gather_cols(
        *[own[i * col_part : (i + 1) * col_part] for i in range(4)]
    )

    def block(gram, position):
        piece = gram[:, position * col_part : (position + 1) * col_part]
        return piece.reshape(modes, piece.shape[2])

    square = (modes, modes)
    pair = (2 * modes, 2 * modes)
    old_stiff = jnp.concatenate([block(gram, 0), block(gram, 1)], 0)
    old_mass = jnp.concatenate([block(gram, 2), block(gram, 3)], 0)
    (ritz_turned,) = dense(first_ritz_kernel, (square,), modes)(
        old_stiff[:modes, :modes], old_mass[:modes, :modes]
    )
    factors = dense(old_kernel, (pair,) * 3, modes)(old_stiff, old_mass)
    for step_index in range(STEPS):
        all_w = (all_kx - edot(ritz_turned, all_mx)) * precond[None, :]
        own_w = lax.dynamic_slice_in_dim(all_w, col_start, col_part, 0)
        received = exchange(own_w, slot_ids, node_count)
        local = apply_local(own_w, tables)
        received, old_mass, factors, local = lax.optimization_barrier(
            (received, old_mass, factors, local)
        )
        space = jnp.concatenate([all_x, all_p, all_w], 0)
        own, part = apply_faces(local, received, blocks, slot_ids, space, dof_count)
        gram = reduce_gram(part)
        stiff_w, mass_w = block(gram, 0), block(gram, 1)
        coeffs, ritz_turned = dense(ritz_kernel, ((modes, 3 * modes), square), modes)(
            stiff_w, mass_w, old_mass, *factors
        )
        if step_index + 1 == STEPS:
            mine = lax.dynamic_slice_in_dim(coeffs, col_start, col_part, 0)
            p_out = edot(mine[:, modes:], space[modes:])
            x_out = p_out + edot(mine[:, :modes], space[:modes])
            return (x_out, p_out, ritz_turned)
        all_kw, all_mw = gather_cols(own[:col_part], own[col_part:])
        wide_x = jnp.concatenate([all_kx, all_mx, all_x], 1)
        wide_rest = jnp.concatenate(
            [
                jnp.concatenate([all_kp, all_mp, all_p], 1),
                jnp.concatenate([all_kw, all_mw, all_w], 1),
            ],
            0,
        )
        new_p = edot(coeffs[:, modes:], wide_rest)
        new_x = new_p + edot(coeffs[:, :modes], wide_x)
        all_kx, all_mx, all_x = [new_x[:, i * row_count : (i + 1) * row_count] for i in range(3)]
        all_p = new_p[:, 2 * row_count :]
        old_mass, *factors = dense(carry_kernel, (pair,) * 4, modes)(
            coeffs, old_stiff, old_mass, stiff_w, mass_w
        )


def solution(mesh):
    rows, cols = mesh.devices.shape
    fine = Mesh(
        mesh.devices.reshape(rows // Y_SIZE, Y_SIZE, cols // CORES, CORES), ROWS + COLS
    )
    placed = (P(COLS, ROWS),) * 2 + (P(ROWS),) * 10
    return jax.shard_map(
        body,
        mesh=fine,
        in_specs=placed,
        out_specs=(P(COLS, ROWS), P(COLS, ROWS), P()),
        check_vma=False,
    )
```

```python
import functools

import jax
import jax.numpy as jnp
from jax import lax
from jax.experimental import pallas as pl
from jax.experimental.pallas import tpu as pltpu
from jax.sharding import Mesh, PartitionSpec as P

ROWS = ("z", "y")
COLS = ("x", "core")
Y_SIZE = 4
CORES = 2
STEPS = 2
RR_ITERS = 3
GROUP = 24


exact_dots = lax.Precision.HIGHEST


def edot(a, b):
    return jnp.dot(a, b, precision=exact_dots)


def swap(array, axis):
    return lax.all_to_all(array, axis, split_axis=0, concat_axis=0, tiled=True)


def spread(array, axis):
    count = lax.axis_size(axis)
    return swap(jnp.broadcast_to(array[None], (count,) + array.shape), axis)


def gather_cols(*blocks):
    count = blocks[0].shape[0]
    moved = lax.all_gather(jnp.concatenate(blocks, 0), COLS, axis=0)
    return [
        moved[:, i * count : (i + 1) * count].reshape(-1, blocks[0].shape[1])
        for i in range(len(blocks))
    ]


def reduce_gram(part):
    piece = jnp.sum(swap(part.reshape(lax.axis_size("y"), -1), "y"), 0)
    piece = jnp.sum(spread(piece, "z"), 0)
    whole = spread(piece, ("y",) + COLS)
    whole = whole.reshape(lax.axis_size("y"), lax.axis_size(COLS), -1, part.shape[1])
    return jnp.swapaxes(whole, 0, 1).reshape((-1,) + part.shape)


def nn(a, b):
    return lax.dot_general(
        a, b, (((1,), (0,)), ((), ())), precision=exact_dots, preferred_element_type=jnp.float32
    )


def nt(a, b):
    return lax.dot_general(
        a, b, (((1,), (1,)), ((), ())), precision=exact_dots, preferred_element_type=jnp.float32
    )


def node_rows(vec_ref, node_ref):
    half = vec_ref.shape[0] // 2
    size = vec_ref.shape[1] // node_ref.shape[0]
    for s in range(node_ref.shape[0]):
        both = [vec_ref[h * half : (h + 1) * half, s * size : (s + 1) * size] for h in range(2)]
        node_ref[s] = jnp.concatenate(both, 1)


def pick_kernel(slot_ref, vec_ref, out_ref, node_ref):
    node_rows(vec_ref, node_ref)
    rows = node_ref.shape[1]

    def group(g, carry):
        first = pl.multiple_of(g * (rows * GROUP), 8)
        pieces = [node_ref[slot_ref[g * GROUP + i]] for i in range(GROUP)]
        out_ref[pl.ds(first, rows * GROUP), :] = jnp.concatenate(pieces, 0)
        return carry

    lax.fori_loop(0, out_ref.shape[0] // (rows * GROUP), group, 0, unroll=2)


def add_product(acc_ref, node, piece, block):
    rows, lanes = piece.shape
    padded = acc_ref.shape[1] // 2
    fill = jnp.zeros((padded - rows, lanes), jnp.float32)
    full = jnp.concatenate([piece, fill], 0)
    half = lanes // 2
    pair = jnp.concatenate([full, pltpu.roll(full, half, 1)], 0)[:, :half]
    high = pair.astype(jnp.bfloat16)
    rest = pair - high.astype(jnp.float32)
    middle = rest.astype(jnp.bfloat16)
    low = (rest - middle.astype(jnp.float32)).astype(jnp.bfloat16)
    terms = jnp.concatenate([high, middle, low], 0)
    out = jnp.dot(terms, block, preferred_element_type=jnp.float32)
    two = 2 * padded
    acc_ref[node] = acc_ref[node] + (out[:two] + out[two : 2 * two] + out[2 * two :])


def local_kernel(dst_ref, src_ref, vec_ref, blocks_ref, acc_ref, node_ref):
    node_rows(vec_ref, node_ref)
    acc_ref[...] = jnp.zeros(acc_ref.shape, jnp.float32)
    first = blocks_ref.shape[0] - src_ref.shape[0]

    def group(g, carry):
        for i in range(GROUP):
            k = g * GROUP + i
            add_product(acc_ref, dst_ref[k], node_ref[src_ref[k]], blocks_ref[first + k])
        return carry

    lax.fori_loop(0, src_ref.shape[0] // GROUP, group, 0)


def face_kernel(
    dof_count, dst_ref, recv_ref, start_ref, blocks_ref, space_ref, own_ref, part_ref, acc_ref
):
    slots = dst_ref.shape[0]
    rows = recv_ref.shape[0] // slots
    nodes, two, lanes = acc_ref.shape
    padded = two // 2
    size = lanes // 2
    acc_ref[...] = start_ref[...]

    def group(g, carry):
        first = pl.multiple_of(g * (rows * GROUP), 8)
        chunk = recv_ref[pl.ds(first, rows * GROUP), :]
        for i in range(GROUP):
            k = g * GROUP + i
            add_product(acc_ref, dst_ref[k], chunk[rows * i : rows * (i + 1)], blocks_ref[k])
        return carry

    lax.fori_loop(0, slots // GROUP, group, 0)
    for which in range(2):
        for h in range(2):
            row = which * 2 * rows + h * rows
            for s in range(nodes):
                own_ref[row : row + rows, s * size : (s + 1) * size] = acc_ref[
                    s, h * padded : h * padded + rows, which * size : (which + 1) * size
                ]
    part_ref[...] = nt(own_ref[...], space_ref[...]) / dof_count


def at(*spaces):
    return [pl.BlockSpec(memory_space=space) for space in spaces]


def exchange(vectors, slot_ids, node_count):
    rows = vectors.shape[0] // 2
    lanes = 2 * vectors.shape[1] // node_count
    picked = pl.pallas_call(
        pick_kernel,
        out_shape=jax.ShapeDtypeStruct((slot_ids.shape[0] * rows, lanes), jnp.float32),
        in_specs=at(pltpu.SMEM, pltpu.VMEM),
        out_specs=at(pltpu.VMEM)[0],
        scratch_shapes=[pltpu.VMEM((node_count, rows, lanes), jnp.float32)],
    )(slot_ids, vectors)
    owners = lax.axis_size(ROWS)
    return swap(picked.reshape(owners, -1), ROWS).reshape(picked.shape)


def apply_local(vectors, tables):
    blocks, src_ids, dst_ids, node_count = tables
    col_count, row_count = vectors.shape
    rows = col_count // 2
    lanes = 2 * row_count // node_count
    padded = -(-rows // 8) * 8
    return pl.pallas_call(
        local_kernel,
        out_shape=jax.ShapeDtypeStruct((node_count, 2 * padded, lanes), jnp.float32),
        in_specs=at(pltpu.SMEM, pltpu.SMEM, pltpu.VMEM, pltpu.VMEM),
        out_specs=at(pltpu.VMEM)[0],
        scratch_shapes=[pltpu.VMEM((node_count, rows, lanes), jnp.float32)],
        compiler_params=pltpu.CompilerParams(vmem_limit_bytes=40 * 2**20),
    )(dst_ids, src_ids, vectors, blocks)


def apply_faces(local, received, blocks, slot_ids, space, dof_count):
    col_count = 2 * received.shape[0] // slot_ids.shape[0]
    shapes = ((2 * col_count, space.shape[1]), (2 * col_count, space.shape[0]))
    return pl.pallas_call(
        functools.partial(face_kernel, dof_count),
        out_shape=tuple(jax.ShapeDtypeStruct(s, jnp.float32) for s in shapes),
        in_specs=at(pltpu.SMEM, *(pltpu.VMEM,) * 4),
        out_specs=at(pltpu.VMEM, pltpu.VMEM),
        scratch_shapes=[pltpu.VMEM(local.shape, jnp.float32)],
        compiler_params=pltpu.CompilerParams(vmem_limit_bytes=40 * 2**20),
    )(slot_ids, received, local, blocks, space)


LANES = 128
PANEL = 8

def lower_inverse(matrix, out_ref):
    size = matrix.shape[0]
    tiles = size // PANEL
    wide = jnp.concatenate([matrix, jnp.zeros((size, LANES - size), jnp.float32)], 1)
    row = lax.broadcasted_iota(jnp.int32, (size, LANES), 0)
    lane = lax.broadcasted_iota(jnp.int32, (size, LANES), 1)
    ident = jnp.where(row == lane, 1.0, 0.0).astype(jnp.float32)
    left = [wide[PANEL * t : PANEL * t + PANEL] for t in range(tiles)]
    right = [ident[PANEL * t : PANEL * t + PANEL] for t in range(tiles)]
    full = (PANEL, LANES)

    def lane_splat(tile, k):
        return jnp.broadcast_to(tile[:, k : k + 1], full)

    def row_splat(tile, i):
        return jnp.broadcast_to(tile[i : i + 1, :], full)

    for p in range(tiles):
        base = PANEL * p
        cols = [lane_splat(left[p], base + k) for k in range(PANEL)]
        s = {(i, k): row_splat(cols[k], i) for k in range(PANEL) for i in range(k, PANEL)}
        rows_l = [row_splat(left[p], i) for i in range(PANEL)]
        rows_r = [row_splat(right[p], i) for i in range(PANEL)]
        later = range(p + 1, min(p + 2, tiles))
        below = {t: [lane_splat(left[t], base + k) for k in range(PANEL)] for t in later}
        lows, roots, outs = [], [], []
        for k in range(PANEL):
            r = lax.rsqrt(s[k, k])
            low = {i: s[i, k] * r for i in range(k + 1, PANEL)}
            for m in range(k + 1, PANEL):
                for i in range(m, PANEL):
                    s[i, m] = s[i, m] - low[i] * low[m]
            new_l = rows_l[k] * r
            new_r = rows_r[k] * r
            out_ref[base + k : base + k + 1, :] = new_r[0:1, :size]
            for i in range(k + 1, PANEL):
                rows_l[i] = rows_l[i] - low[i] * new_l
                rows_r[i] = rows_r[i] - low[i] * new_r
            for t in later:
                factor = below[t][k] * r
                for i in range(k + 1, PANEL):
                    below[t][i] = below[t][i] - low[i] * factor
                left[t] = left[t] - factor * new_l
                right[t] = right[t] - factor * new_r
            lows.append(low)
            roots.append(r)
            outs.append((new_l, new_r))
        for t in range(p + 2, tiles):
            factors = [lane_splat(left[t], base + k) for k in range(PANEL)]
            for k in range(PANEL):
                factors[k] = factors[k] * roots[k]
                for i in range(k + 1, PANEL):
                    factors[i] = factors[i] - lows[k][i] * factors[k]
                left[t] = left[t] - factors[k] * outs[k][0]
                right[t] = right[t] - factors[k] * outs[k][1]


def first_ritz_kernel(stiff_ref, mass_ref, ritz_ref, tmp_ref):
    lower_inverse(mass_ref[...], tmp_ref)
    inv = tmp_ref[...]
    ritz_ref[...] = nn(nt(stiff_ref[...], inv), inv)


def factor_old(stiff, mass, j_ref, jm_ref, b_ref, tmp_ref):
    n = tmp_ref.shape[0]
    lower_inverse(stiff[:n, :n], tmp_ref)
    first = tmp_ref[...]
    q = nt(stiff[n:, :n], first)
    lower_inverse(stiff[n:, n:] - nt(q, q), tmp_ref)
    second = tmp_ref[...]
    j_ref[:n, :n] = first
    j_ref[:n, n:] = jnp.zeros((n, n), jnp.float32)
    j_ref[n:, :n] = -nn(second, nn(q, first))
    j_ref[n:, n:] = second
    j = j_ref[...]
    jm = nt(mass, j)
    jm_ref[...] = jm
    b_ref[...] = nn(j, jm)


def old_kernel(stiff_ref, mass_ref, j_ref, jm_ref, b_ref, tmp_ref):
    factor_old(stiff_ref[...], mass_ref[...], j_ref, jm_ref, b_ref, tmp_ref)


def carry_kernel(
    y_ref, gxp_ref, mxp_ref, gw_ref, mw_ref, next_ref, j_ref, jm_ref, b_ref, tmp_ref
):
    n = tmp_ref.shape[0]
    ya = y_ref[:, : 2 * n]
    yb = y_ref[:, 2 * n :]
    lane = lax.broadcasted_iota(jnp.int32, ya.shape, 1)
    pa = jnp.concatenate([ya, jnp.where(lane < n, 0.0, ya)], 0)
    pb = jnp.concatenate([yb, yb], 0)

    def turned(old_ref, col_ref):
        col = col_ref[:, : 2 * n]
        ha = nn(pa, old_ref[...]) + nn(pb, col)
        hb = nt(pa, col) + nn(pb, col_ref[:, 2 * n :])
        return nt(ha, pa) + nt(hb, pb)

    mass = turned(mxp_ref, mw_ref)
    next_ref[...] = mass
    factor_old(turned(gxp_ref, gw_ref), mass, j_ref, jm_ref, b_ref, tmp_ref)


def ritz_kernel(
    gw_ref, mw_ref, mxp_ref, j_ref, jm_ref, b_ref, y_ref, ritz_ref, tmp_ref
):
    n = tmp_ref.shape[0]
    j = j_ref[...]
    bxx = b_ref[...]
    qt = nt(gw_ref[:, : 2 * n], j)
    lower_inverse(gw_ref[:, 2 * n :] - nt(qt, qt), tmp_ref)
    lw = tmp_ref[...]
    t = nn(qt, j)
    mwx = mw_ref[:, : 2 * n]
    d = mwx - nn(t, mxp_ref[...])
    e = mw_ref[:, 2 * n :] - nt(t, mwx) - nt(d, t)
    bwx = nn(lw, nt(d, j))
    bww = nt(nn(lw, e), lw)
    va = jm_ref[:n, :]
    vb = jnp.transpose(nn(lw, d[:, :n]))
    ua = ub = None
    for inner_index in range(RR_ITERS):
        wa = nn(va, bxx) + nn(vb, bwx)
        wb = nt(va, bwx) + nn(vb, bww)
        lower_inverse(nt(wa, va) + nt(wb, vb), tmp_ref)
        lc = tmp_ref[...]
        ua, ub = nn(lc, va), nn(lc, vb)
        va, vb = nn(lc, wa), nn(lc, wb)
    ritz_ref[...] = nt(ua, ua) + nt(ub, ub)
    yw = nn(ub, lw)
    y_ref[:, : 2 * n] = nn(ua, j) - nn(yw, t)
    y_ref[:, 2 * n :] = yw


def dense(kernel, shapes, size):
    return pl.pallas_call(
        kernel,
        out_shape=tuple(jax.ShapeDtypeStruct(s, jnp.float32) for s in shapes),
        scratch_shapes=[pltpu.VMEM((size, size), jnp.float32)],
    )


def body(
    x_start,
    p_start,
    k_diag,
    k_link,
    m_diag,
    m_link,
    link_to,
    link_count,
    k_iface,
    m_iface,
    iface_local,
    iface_live,
):
    col_part, row_count = x_start.shape
    modes = col_part * lax.axis_size(COLS)
    dof_count = row_count * lax.axis_size(ROWS)
    node_count, link_slots = link_to.shape
    node_size = k_diag.shape[1]
    node_ids = jnp.arange(node_count, dtype=jnp.int32)
    slot_ids = iface_local.reshape(-1)
    slot_live = iface_live.reshape(-1) > 0
    link_live = jnp.arange(link_slots, dtype=jnp.int32)[None, :] < link_count[:, None]

    def side_by_side(k_part, m_part, live):
        pair = jnp.concatenate([k_part, m_part], 2)
        return jnp.where(live[:, None, None], pair, jnp.zeros_like(pair))

    def flat(blocks):
        return blocks.reshape(-1, node_size, node_size)

    def flipped(blocks):
        return jnp.swapaxes(flat(blocks), 1, 2)

    live_flat = link_live.reshape(-1)
    blocks = jnp.concatenate(
        [
            side_by_side(flat(k_iface), flat(m_iface), slot_live),
            side_by_side(k_diag, m_diag, jnp.ones((node_count,), bool)),
            side_by_side(flipped(k_link), flipped(m_link), live_flat),
            side_by_side(flat(k_link), flat(m_link), live_flat),
        ],
        0,
    )
    link_from = jnp.repeat(node_ids, link_slots)
    link_flat = link_to.reshape(-1)
    src_ids = jnp.concatenate([node_ids, link_flat, link_from])
    dst_ids = jnp.concatenate([node_ids, link_from, link_flat])
    tables = (blocks, src_ids, dst_ids, node_count)

    precond = 1.0 / jnp.diagonal(k_diag.astype(jnp.float32), axis1=1, axis2=2).reshape(-1)
    col_start = lax.axis_index(COLS) * col_part

    start = jnp.concatenate([x_start, p_start], 0)
    received = exchange(start, slot_ids, node_count)
    all_x, all_p = gather_cols(x_start, p_start)
    local = apply_local(start, tables)
    space = jnp.concatenate([all_x, all_p], 0)
    own, part = apply_faces(local, received, blocks, slot_ids, space, dof_count)
    gram = reduce_gram(part)
    all_kx, all_kp, all_mx, all_mp = gather_cols(
        *[own[i * col_part : (i + 1) * col_part] for i in range(4)]
    )

    def block(gram, position):
        piece = gram[:, position * col_part : (position + 1) * col_part]
        return piece.reshape(modes, piece.shape[2])

    square = (modes, modes)
    pair = (2 * modes, 2 * modes)
    old_stiff = jnp.concatenate([block(gram, 0), block(gram, 1)], 0)
    old_mass = jnp.concatenate([block(gram, 2), block(gram, 3)], 0)
    (ritz_turned,) = dense(first_ritz_kernel, (square,), modes)(
        old_stiff[:modes, :modes], old_mass[:modes, :modes]
    )
    factors = dense(old_kernel, (pair,) * 3, modes)(old_stiff, old_mass)
    for step_index in range(STEPS):
        all_w = (all_kx - edot(ritz_turned, all_mx)) * precond[None, :]
        own_w = lax.dynamic_slice_in_dim(all_w, col_start, col_part, 0)
        received = exchange(own_w, slot_ids, node_count)
        local = apply_local(own_w, tables)
        received, old_mass, factors, local = lax.optimization_barrier(
            (received, old_mass, factors, local)
        )
        space = jnp.concatenate([all_x, all_p, all_w], 0)
        own, part = apply_faces(local, received, blocks, slot_ids, space, dof_count)
        gram = reduce_gram(part)
        stiff_w, mass_w = block(gram, 0), block(gram, 1)
        coeffs, ritz_turned = dense(ritz_kernel, ((modes, 3 * modes), square), modes)(
            stiff_w, mass_w, old_mass, *factors
        )
        if step_index + 1 == STEPS:
            mine = lax.dynamic_slice_in_dim(coeffs, col_start, col_part, 0)
            p_out = edot(mine[:, modes:], space[modes:])
            x_out = p_out + edot(mine[:, :modes], space[:modes])
            return (x_out, p_out, ritz_turned)
        all_kw, all_mw = gather_cols(own[:col_part], own[col_part:])
        wide_x = jnp.concatenate([all_kx, all_mx, all_x], 1)
        wide_rest = jnp.concatenate(
            [
                jnp.concatenate([all_kp, all_mp, all_p], 1),
                jnp.concatenate([all_kw, all_mw, all_w], 1),
            ],
            0,
        )
        new_p = edot(coeffs[:, modes:], wide_rest)
        new_x = new_p + edot(coeffs[:, :modes], wide_x)
        all_kx, all_mx, all_x = [new_x[:, i * row_count : (i + 1) * row_count] for i in range(3)]
        all_p = new_p[:, 2 * row_count :]
        old_mass, *factors = dense(carry_kernel, (pair,) * 4, modes)(
            coeffs, old_stiff, old_mass, stiff_w, mass_w
        )


def solution(mesh):
    rows, cols = mesh.devices.shape
    fine = Mesh(
        mesh.devices.reshape(rows // Y_SIZE, Y_SIZE, cols // CORES, CORES), ROWS + COLS
    )
    placed = (P(COLS, ROWS),) * 2 + (P(ROWS),) * 10
    return jax.shard_map(
        body,
        mesh=fine,
        in_specs=placed,
        out_specs=(P(COLS, ROWS), P(COLS, ROWS), P()),
        check_vma=False,
    )
```
